32 devices in a mesh: groups: 2 (over y), gcol: 8 (over z, x), grow: 2 (over core).
Axes of the slice: x: 2, y: 2, z: 4, core: 2. Of those that a mesh axis runs over, the one named last changes fastest.
Arguments:
- patches: bfloat16 [16, 256, 1024], P(('groups', 'grow'), 'gcol'), parts along dimension 0, may hold values from -6 to 6
- mask_token: bfloat16 [1024], replicated, may hold values from -6 to 6
- masked: int32 [16, 256], P(('groups', 'grow'), 'gcol'), parts along dimension 0, may hold values 0 or 1
- tissue: int32 [16, 256], P(('groups', 'grow'), 'gcol'), parts along dimension 0, may hold values 0 or 1
- in_weight: bfloat16 [2304, 1024], P(None, 'grow'), may hold values from -0.1875 to 0.1875
- out_weight: bfloat16 [1024, 1024], P(None, 'grow'), may hold values from -0.1875 to 0.1875
- row_decay: float32 [8, 16, 256], P(None, ('groups', 'grow'), 'gcol'), parts along dimension 1, may hold values from -1.5 to 0
- col_decay: float32 [8, 16, 256], P(None, ('groups', 'grow'), 'gcol'), parts along dimension 1, may hold values from -1.5 to 0
- cotangent: bfloat16 [16, 256, 1024], P(('groups', 'grow'), 'gcol'), parts along dimension 0, may hold values from -6 to 6
Outputs:
- patch_grad: bfloat16 [16, 256, 1024], P(('groups', 'grow'), 'gcol'), parts along dimension 0
- out_weight_grad: float32 [2048, 1024], P(('groups', 'gcol', 'grow')), parts along dimension 0
The draws below stay inside these ranges and needn't reach their ends.
There are 2 independent parts, one for each index of `groups`. The reference program is written for one: setup_inputs(seed, part) draws one part's arguments, and reference() takes and returns one part's arrays. A program takes and returns all parts, laid end to end along the dimension named above; an argument that names none is the same for every part. Nothing has to cross between parts.
All inputs are finite; a program needn't handle non-finite values. No bound on the sum of `masked` or of `tissue` on one device may be relied on, other than what follows from the above.
Results may differ from the reference program's by a relative error of at most 0.0095.
The reference program's roundings to bfloat16 on the way count: a program that leaves them out, or rounds other values in their place, can miss the bound.
Values may be sent and summed in bfloat16 or wider, within the bound.
A program may use at most 320 MiB of HBM per device.

```python
import math
import jax
import jax.numpy as jnp
from jax import lax

D = 1024
E = 1024
HEADS = 16
N = 64
CH = 4
CW = 32
PATCH_GRID_ROWS = 8
PATCH_GRID_COLS = 256


def decay_field(key, sequence_length):
    number_of_heads = HEADS // 2
    random_split_keys = jax.random.split(key, 7)
    ranking = jax.random.permutation(random_split_keys[0], number_of_heads)
    slow_count = number_of_heads // 2
    is_slow = ranking < slow_count
    slow_rate = jax.random.uniform(random_split_keys[1], (number_of_heads,), jnp.float32, 0.1, 0.4) * (math.log(10.0) / sequence_length)
    fast_rate = jax.random.uniform(random_split_keys[2], (number_of_heads,), jnp.float32, 1.0 / 50.0, 1.0 / 30.0)
    base_rate = jnp.where(is_slow, slow_rate, fast_rate)
    blocks = jax.random.uniform(random_split_keys[3], (number_of_heads, PATCH_GRID_ROWS // CH, PATCH_GRID_COLS // CW), jnp.float32, -0.5, 0.5)
    blocks = jnp.repeat(jnp.repeat(blocks, CH, axis=1), CW, axis=2)
    jitter = jax.random.uniform(random_split_keys[4], (number_of_heads, PATCH_GRID_ROWS, PATCH_GRID_COLS), jnp.float32, -0.35, 0.35)
    spike_position = jax.random.randint(random_split_keys[5], (number_of_heads, PATCH_GRID_ROWS, PATCH_GRID_COLS), 0, sequence_length) < 2
    spike_loss_value = jax.random.uniform(random_split_keys[6], (number_of_heads, PATCH_GRID_ROWS, PATCH_GRID_COLS), jnp.float32, 0.22, 0.69)
    stable_baseline = base_rate[:, None, None] * jnp.exp(blocks + jitter)
    return -stable_baseline - jnp.where(spike_position, spike_loss_value, 0.0)


def draw_row_decay(key, part):
    return decay_field(jax.random.fold_in(key, 7), PATCH_GRID_COLS)


def draw_col_decay(key, part):
    return decay_field(jax.random.fold_in(key, 11), PATCH_GRID_ROWS)


def place_ends(array, own_key, smallest, high):
    place = [jax.random.randint(jax.random.fold_in(own_key, axis), (), 0, length) for axis, length in enumerate(array.shape)]
    longest = array.shape.index(max(array.shape))
    next_to = place[:longest] + [(place[longest] + 1) % array.shape[longest]] + place[longest + 1:]
    return array.at[tuple(place)].set(smallest).at[tuple(next_to)].set(high)


def spiked(drawn, rng, source, target, parts, factor):
    owner, partner = [(jnp.arange(drawn.shape[position]) // (drawn.shape[position] // parts)).reshape([-1 if axis == position else 1 for axis in range(drawn.ndim)]) for position in (source, target)]
    chosen = jax.random.permutation(rng, parts)[partner]
    strong = (owner == chosen) | (owner == (partner + parts // 2) % parts)
    return jnp.where(strong, factor * drawn, drawn)


def block_levels(stream_key, dims, shards, least, largest):
    loudness, own = 1.0, jax.random.fold_in(stream_key, 6)
    for position, blocks in shards:
        steps = jnp.exp(jax.random.uniform(jax.random.fold_in(own, position), (blocks,), jnp.float32, least / len(shards), largest / len(shards)))
        loudness = loudness * jnp.repeat(steps, dims[position] // blocks).reshape([-1 if axis == position else 1 for axis in range(len(dims))])
    return loudness


def bell_draw(stream_key, shape, width, bound, cuts=(), kind=jnp.bfloat16):
    array = jax.random.normal(stream_key, shape, jnp.float32) * width
    if len(cuts) > 0:
        array = block_levels(stream_key, shape, cuts, -0.22, 0.18) * array
    return jnp.clip(array, min=-bound, max=bound).astype(kind)


def bell_draw_with(own_key, extent, scale, limit, cuts, heavy, held_as=jnp.bfloat16):
    drawn = scale * jax.random.normal(own_key, extent, jnp.float32)
    if cuts:
        drawn = drawn * block_levels(own_key, extent, cuts, -0.22, 0.18)
    return jnp.clip(spiked(drawn, jax.random.fold_in(own_key, 3), *heavy), -limit, limit).astype(held_as)


def setup_inputs(seed: int = 0, part: int = 0) -> dict:
    splits = jax.random.split(jax.random.key(seed), 10)
    own_keys = jax.random.split(jax.random.fold_in(splits[9], part), 10)
    return {
        "patches": bell_draw(own_keys[0], (PATCH_GRID_ROWS, PATCH_GRID_COLS, D), 1.0, 6.0, ((0, 2), (1, 8))),
        "mask_token": bell_draw(splits[1], (D,), 1.0, 6.0),
        "masked": place_ends((jax.random.randint(own_keys[2], (PATCH_GRID_ROWS, PATCH_GRID_COLS), 0, 4) < 3).astype(jnp.int32), jax.random.fold_in(own_keys[2], 1), 0, 1),
        "tissue": place_ends((jax.random.randint(own_keys[3], (PATCH_GRID_ROWS, PATCH_GRID_COLS), 0, 5) < 4).astype(jnp.int32), jax.random.fold_in(own_keys[3], 1), 0, 1),
        "in_weight": bell_draw(splits[4], (2 * E + 4 * N, D), D ** -0.5, 0.1875, ((1, 2),)),
        "out_weight": bell_draw(splits[5], (D, E), E ** -0.5, 0.1875, ((1, 2),)),
        "row_decay": draw_row_decay(jax.random.fold_in(jax.random.fold_in(splits[9], part), 71), part),
        "col_decay": draw_col_decay(jax.random.fold_in(jax.random.fold_in(splits[9], part), 71), part),
        "cotangent": bell_draw_with(own_keys[8], (PATCH_GRID_ROWS, PATCH_GRID_COLS, D), 1.0, 6.0, ((0, 2), (1, 8)), (1, 2, 8, 2.0)),
    }


EPSILON = 1e-05
PRECISE = lax.Precision.HIGHEST

def scan_lines(inputs, key_vecs, query_vecs, log_decay):
    line_count, length, number_of_heads, head_size = inputs.shape
    state_size = key_vecs.shape[2]
    block_len = math.gcd(length, 64)
    block_count = length // block_len
    pieces_in = inputs.reshape(line_count, block_count, block_len, number_of_heads, head_size).transpose(1, 0, 2, 3, 4)
    pieces_key = key_vecs.reshape(line_count, block_count, block_len, state_size).transpose(1, 0, 2, 3)
    pieces_query = query_vecs.reshape(line_count, block_count, block_len, state_size).transpose(1, 0, 2, 3)
    pieces_log = log_decay.reshape(number_of_heads, line_count, block_count, block_len).transpose(2, 0, 1, 3)
    causal = jnp.arange(block_len)[:, None] >= jnp.arange(block_len)[None, :]

    def block_step(state_now, pieces):
        piece_in, piece_key, piece_query, piece_log = pieces
        running = jnp.cumsum(piece_log, axis=2)
        whole_log = running[:, :, -1]
        log_gaps = running[:, :, :, None] - running[:, :, None, :]
        decay_mat = jnp.where(causal, jnp.exp(jnp.where(causal, log_gaps, 0.0)), 0.0)
        scores = jnp.einsum('ltn,lkn->ltk', piece_query, piece_key, precision=PRECISE)
        within = jnp.einsum('gltk,lkgp->ltgp', decay_mat * scores[None], piece_in, precision=PRECISE)
        carried = jnp.einsum('ltn,lgpn->ltgp', piece_query, state_now, precision=PRECISE)
        carried = carried * jnp.exp(running).transpose(1, 2, 0)[..., None]
        to_end = jnp.exp(whole_log[:, :, None] - running)
        fresh = jnp.einsum('glk,lkgp,lkn->lgpn', to_end, piece_in, piece_key, precision=PRECISE)
        state_next = jnp.exp(whole_log).T[:, :, None, None] * state_now + fresh
        return (state_next, within + carried)
    start_state = jnp.zeros((line_count, number_of_heads, head_size, state_size), jnp.float32)
    final_state, outputs = lax.scan(block_step, start_state, (pieces_in, pieces_key, pieces_query, pieces_log))
    return outputs.transpose(1, 0, 2, 3, 4).reshape(line_count, length, number_of_heads, head_size)

def layer_forward(model_in, in_weight, out_weight, row_decay, col_decay):
    grid_rows, grid_cols, feat_width = model_in.shape
    tok_count = grid_rows * grid_cols
    inner_width = out_weight.shape[1]
    half_width = inner_width // 2
    state_size = (in_weight.shape[0] - 2 * inner_width) // 4
    number_of_heads = HEADS // 2
    head_size = inner_width // HEADS
    projected = jnp.dot(model_in.reshape(tok_count, feat_width), in_weight.T, preferred_element_type=jnp.float32)
    proj_bf = projected.astype(jnp.bfloat16)
    pre_values = proj_bf[:, :inner_width].astype(jnp.float32)
    gate_pre = proj_bf[:, inner_width:2 * inner_width].astype(jnp.float32)
    offset = 2 * inner_width
    key_rows = proj_bf[:, offset:offset + state_size].astype(jnp.float32).reshape(grid_rows, grid_cols, state_size)
    query_rows = proj_bf[:, offset + state_size:offset + 2 * state_size].astype(jnp.float32).reshape(grid_rows, grid_cols, state_size)
    key_cols = proj_bf[:, offset + 2 * state_size:offset + 3 * state_size].astype(jnp.float32).reshape(grid_rows, grid_cols, state_size).transpose(1, 0, 2)
    query_cols = proj_bf[:, offset + 3 * state_size:offset + 4 * state_size].astype(jnp.float32).reshape(grid_rows, grid_cols, state_size).transpose(1, 0, 2)
    values = jax.nn.silu(pre_values)
    row_inputs = values[:, :half_width].reshape(grid_rows, grid_cols, number_of_heads, head_size)
    col_inputs = values[:, half_width:].reshape(grid_rows, grid_cols, number_of_heads, head_size).transpose(1, 0, 2, 3)
    row_out = scan_lines(row_inputs, key_rows, query_rows, row_decay)
    col_out = scan_lines(col_inputs, key_cols, query_cols, col_decay.transpose(0, 2, 1)).transpose(1, 0, 2, 3)
    mixed = jnp.concatenate([row_out.reshape(tok_count, half_width), col_out.reshape(tok_count, half_width)], axis=1)
    gated = (mixed * jax.nn.silu(gate_pre)).reshape(tok_count, HEADS, head_size)
    normed = gated * lax.rsqrt(lax.optimization_barrier(jnp.mean(gated * gated, axis=2, keepdims=True)) + EPSILON)
    normed_bf = normed.reshape(tok_count, inner_width).astype(jnp.bfloat16)
    layer_out = jnp.dot(normed_bf, out_weight.T, preferred_element_type=jnp.float32)
    return (layer_out, normed_bf)

def reference(patches, mask_token, masked, tissue, in_weight, out_weight, row_decay, col_decay, cotangent):
    grid_rows, grid_cols, feat_width = patches.shape
    tok_count = grid_rows * grid_cols
    chosen = (masked == 1)[:, :, None]
    present = tissue.astype(jnp.bfloat16)[:, :, None]
    model_in = jnp.where(chosen, mask_token[None, None, :], patches) * present
    grad_out = cotangent * masked.astype(jnp.bfloat16)[:, :, None]
    grad_flat = grad_out.reshape(tok_count, feat_width)

    def forward(value):
        return layer_forward(value, in_weight, out_weight, row_decay, col_decay)
    layer_out, pullback, normed_bf = jax.vjp(forward, model_in, has_aux=True)
    grad_model_in, = pullback(grad_flat.astype(jnp.float32))
    keep_mask = present * (1 - masked).astype(jnp.bfloat16)[:, :, None]
    patch_grad = grad_model_in.astype(jnp.bfloat16) * keep_mask
    weight_sum = jnp.dot(grad_flat.T, normed_bf, preferred_element_type=jnp.float32)
    out_weight_grad = weight_sum * (1.0 / math.sqrt(tok_count))
    return (patch_grad, out_weight_grad)
```

```python
import functools
import math

import jax
import jax.numpy as jnp
from jax import lax
from jax.experimental import pallas as pl
from jax.experimental.pallas import tpu as pltpu
from jax.sharding import PartitionSpec as P

E = 1024
HEADS = 16
N = 64


EPSILON = 1e-05
PRECISE = lax.Precision.HIGHEST


def prefix(value, axis, join, neutral):
    count, mine = (lax.axis_size(axis), lax.axis_index(axis))
    pieces = jax.tree.map(lambda part: lax.all_gather(part, axis), value)
    so_far = jax.tree.map(
        lambda part, zero: jnp.full_like(part, 0) + jnp.asarray(zero, part.dtype), value, neutral
    )

    def prefix_hop(position, so_far):
        longer = join(so_far, jax.tree.map(lambda part: part[position], pieces))
        return jax.tree.map(lambda new, old: jnp.where(position < mine, new, old), longer, so_far)

    return lax.fori_loop(0, count - 1, prefix_hop, so_far)


def carried_in(shard, axis, combine, identity):
    length, position = (lax.axis_size(axis), lax.axis_index(axis))
    everything = jax.tree.map(
        lambda part, kind: lax.all_gather(part.astype(kind), axis),
        shard,
        jax.tree.map(lambda a: jnp.bfloat16 if a.dtype == jnp.float32 else a.dtype, shard),
    )
    start = jax.tree.map(
        lambda part, zero: jnp.broadcast_to(jnp.asarray(zero, part.dtype), part.shape),
        shard,
        identity,
    )

    def carried_hop(k, before):
        at = length - 1 - k
        reached = at > position
        new = combine(
            before, jax.tree.map(lambda part, own: part[at].astype(own.dtype), everything, shard)
        )
        return jax.tree.map(lambda a, b: jnp.where(reached, a, b), new, before)

    return lax.fori_loop(0, length, carried_hop, start)


def shortened(shard):

    def short(part):
        return part.astype(jnp.bfloat16) if part.dtype == jnp.float32 else part

    return jax.tree.map(short, shard)


def silu_grad(pre_act):
    sigmoid_v = jax.nn.sigmoid(pre_act)
    return sigmoid_v * (1.0 + pre_act * (1.0 - sigmoid_v))


def per_channel(head_part, channels):
    return jnp.repeat(head_part, channels // head_part.shape[-1], axis=-1)


def line_form(head_lines, channels):
    return per_channel(head_lines.transpose(1, 2, 0), channels)


def carry_on(log_lines, state):
    return per_channel(jnp.exp(log_lines), state.shape[2])[:, None, :] * state


def prepare(log_decay):
    length = log_decay.shape[2]
    running = jnp.cumsum(log_decay, axis=2)
    whole_log = running[:, :, -1]
    causal = jnp.arange(length)[:, None] >= jnp.arange(length)[None, :]
    log_gaps = running[:, :, :, None] - running[:, :, None, :]
    decay_mat = jnp.where(causal, jnp.exp(jnp.where(causal, log_gaps, 0.0)), 0.0)
    return (running, whole_log, decay_mat)


def chain_link(earlier, later):
    return (earlier[0] + later[0], carry_on(later[0], earlier[1]) + later[1])


def split_heads(lines, head_count):
    line_count, length, channels = lines.shape
    return lines.reshape(line_count, length, head_count, channels // head_count)


def local_summary(inputs, key_vecs, prepared):
    running, whole_log, decay_mat = prepared
    to_end = line_form(jnp.exp(whole_log[:, :, None] - running), inputs.shape[2])
    fresh = jnp.einsum("ltc,ltn->lnc", inputs * to_end, key_vecs, precision=PRECISE)
    return (whole_log.T, fresh)


def local_return(query_vecs, prepared, upstream):
    running, whole_log, decay_mat = prepared
    from_start = line_form(jnp.exp(running), upstream.shape[2])
    backward = jnp.einsum("ltc,ltn->lnc", upstream * from_start, query_vecs, precision=PRECISE)
    return (whole_log.T, backward)


def local_outputs(inputs, key_vecs, query_vecs, prepared, incoming):
    running, whole_log, decay_mat = prepared
    head_count = decay_mat.shape[0]
    line_count, length, channels = inputs.shape
    scores = jnp.einsum("ltn,lkn->ltk", query_vecs, key_vecs, precision=PRECISE)
    within = jnp.einsum(
        "gltk,lkgp->ltgp",
        decay_mat * scores[None],
        split_heads(inputs, head_count),
        precision=PRECISE,
    )
    within = within.reshape(line_count, length, channels)
    carried = jnp.einsum("ltn,lnc->ltc", query_vecs, incoming, precision=PRECISE)
    return within + carried * line_form(jnp.exp(running), channels)


def local_grads(inputs, key_vecs, query_vecs, prepared, incoming, returning, upstream):
    running, whole_log, decay_mat = prepared
    head_count = decay_mat.shape[0]
    line_count, length, channels = inputs.shape
    from_start = line_form(jnp.exp(running), channels)
    to_end = line_form(jnp.exp(whole_log[:, :, None] - running), channels)
    scores = jnp.einsum("ltn,lkn->ltk", query_vecs, key_vecs, precision=PRECISE)
    heads_up = split_heads(upstream, head_count)
    heads_in = split_heads(inputs, head_count)
    grad_inputs = jnp.einsum(
        "gltk,ltgp->lkgp", decay_mat * scores[None], heads_up, precision=PRECISE
    ).reshape(line_count, length, channels)
    grad_inputs = (
        grad_inputs + jnp.einsum("lnc,lkn->lkc", returning, key_vecs, precision=PRECISE) * to_end
    )
    mixed = jnp.einsum("ltgp,lkgp->gltk", heads_up, heads_in, precision=PRECISE) * decay_mat
    grad_keys = jnp.einsum("gltk,ltn->lkn", mixed, query_vecs, precision=PRECISE)
    grad_keys = grad_keys + jnp.einsum(
        "lkc,lnc->lkn", inputs * to_end, returning, precision=PRECISE
    )
    grad_queries = jnp.einsum("gltk,lkn->ltn", mixed, key_vecs, precision=PRECISE)
    grad_queries = grad_queries + jnp.einsum(
        "ltc,lnc->ltn", upstream * from_start, incoming, precision=PRECISE
    )
    return (grad_inputs, grad_keys, grad_queries)


def shards(
    patches, mask_token, masked, tissue, in_weight, out_weight, row_decay, col_decay, cotangent
):
    grid_rows, grid_cols, feat_width = patches.shape
    tok_count = grid_rows * grid_cols
    chosen = (masked == 1)[:, :, None]
    present = tissue.astype(jnp.bfloat16)[:, :, None]
    model_in = jnp.where(chosen, mask_token[None, None, :], patches) * present
    flat_in = model_in.reshape(tok_count, feat_width)
    inner_width = E
    half_width = inner_width // 2
    state_size = N
    number_of_heads = HEADS // 2
    offset = 2 * inner_width
    full_in, full_out = (
        lax.all_gather(in_weight, "grow", axis=1, tiled=True),
        lax.all_gather(out_weight, "grow", axis=1, tiled=True),
    )
    projected = lax.dot_general(
        flat_in, full_in, (((1,), (1,)), ((), ())), preferred_element_type=jnp.float32
    )
    proj_bf = projected.astype(jnp.bfloat16)
    pre_values = proj_bf[:, :inner_width].astype(jnp.float32)
    gate_pre = proj_bf[:, inner_width:offset].astype(jnp.float32)
    key_rows = (
        proj_bf[:, offset : offset + state_size]
        .astype(jnp.float32)
        .reshape(grid_rows, grid_cols, state_size)
    )
    query_rows = (
        proj_bf[:, offset + state_size : offset + 2 * state_size]
        .astype(jnp.float32)
        .reshape(grid_rows, grid_cols, state_size)
    )
    key_cols = (
        proj_bf[:, offset + 2 * state_size : offset + 3 * state_size]
        .astype(jnp.float32)
        .reshape(grid_rows, grid_cols, state_size)
        .transpose(1, 0, 2)
    )
    query_cols = (
        proj_bf[:, offset + 3 * state_size : offset + 4 * state_size]
        .astype(jnp.float32)
        .reshape(grid_rows, grid_cols, state_size)
        .transpose(1, 0, 2)
    )
    values = jax.nn.silu(pre_values)
    row_inputs = values[:, :half_width].reshape(grid_rows, grid_cols, half_width)
    col_inputs = values[:, half_width:].reshape(grid_rows, grid_cols, half_width).transpose(1, 0, 2)
    row_prep = prepare(row_decay)
    col_prep = prepare(col_decay.transpose(0, 2, 1))
    row_zero = (
        jnp.zeros((grid_rows, number_of_heads), jnp.float32),
        jnp.zeros((grid_rows, state_size, half_width), jnp.float32),
    )
    col_zero = (
        jnp.zeros((grid_cols, number_of_heads), jnp.float32),
        jnp.zeros((grid_cols, state_size, half_width), jnp.float32),
    )
    row_entry = prefix(local_summary(row_inputs, key_rows, row_prep), "gcol", chain_link, row_zero)[
        1
    ]
    grow_size = lax.axis_size("grow")
    my_block = lax.axis_index("grow")
    parts_in, parts_key, parts_log = (
        lax.all_gather(
            proj_bf[:, half_width:inner_width].reshape(grid_rows, grid_cols, half_width),
            "grow",
            axis=0,
            tiled=True,
        ),
        lax.all_gather(
            proj_bf[:, offset + 2 * state_size : offset + 3 * state_size].reshape(
                grid_rows, grid_cols, state_size
            ),
            "grow",
            axis=0,
            tiled=True,
        ),
        lax.all_gather(
            col_decay.transpose(1, 0, 2).astype(jnp.bfloat16), "grow", axis=0, tiled=True
        ).astype(jnp.float32),
    )
    col_entry = col_zero[1]
    for block_idx in range(grow_size):
        lower_row = block_idx * grid_rows
        piece_in = jax.nn.silu(
            parts_in[lower_row : lower_row + grid_rows].astype(jnp.float32)
        ).transpose(1, 0, 2)
        piece_keys = (
            parts_key[lower_row : lower_row + grid_rows].astype(jnp.float32).transpose(1, 0, 2)
        )
        piece_log = parts_log[lower_row : lower_row + grid_rows].transpose(1, 2, 0)
        whole_log, piece_state = local_summary(piece_in, piece_keys, prepare(piece_log))
        moved = carry_on(whole_log, col_entry) + piece_state
        col_entry = jnp.where(block_idx < my_block, moved, col_entry)
    row_out = local_outputs(row_inputs, key_rows, query_rows, row_prep, row_entry)
    col_out = local_outputs(col_inputs, key_cols, query_cols, col_prep, col_entry).transpose(
        1, 0, 2
    )
    mixed = jnp.concatenate(
        [row_out.reshape(tok_count, half_width), col_out.reshape(tok_count, half_width)], axis=1
    )
    gate_act = jax.nn.silu(gate_pre)
    head_size = inner_width // HEADS
    gated = (mixed * gate_act).reshape(tok_count, HEADS, head_size)
    inv_rms = lax.rsqrt(jnp.mean(gated * gated, axis=2, keepdims=True) + EPSILON)
    normed = gated * inv_rms
    normed_bf = normed.reshape(tok_count, inner_width).astype(jnp.bfloat16)
    grad_out = (cotangent * masked.astype(jnp.bfloat16)[:, :, None]).reshape(tok_count, feat_width)
    total_patches = tok_count * lax.axis_size("gcol") * lax.axis_size("grow")
    weight_sum = lax.psum_scatter(
        lax.dot_general(
            grad_out, normed_bf, (((0,), (0,)), ((), ())), preferred_element_type=jnp.float32
        ),
        ("gcol", "grow"),
        scatter_dimension=0,
        tiled=True,
    )
    out_weight_grad = weight_sum * (1.0 / math.sqrt(total_patches))
    grad_normed_bf = jnp.dot(grad_out, full_out, preferred_element_type=jnp.float32).astype(
        jnp.bfloat16
    )
    grad_normed = lax.optimization_barrier(grad_normed_bf).astype(jnp.float32)
    grad_normed = grad_normed.reshape(tok_count, HEADS, head_size)
    grad_gated = inv_rms * (
        grad_normed - normed * jnp.mean(grad_normed * normed, axis=2, keepdims=True)
    )
    grad_gated = grad_gated.reshape(tok_count, inner_width)
    grad_mixed = grad_gated * gate_act
    grad_gate = grad_gated * mixed * silu_grad(gate_pre)
    row_up = grad_mixed[:, :half_width].reshape(grid_rows, grid_cols, half_width)
    col_up = grad_mixed[:, half_width:].reshape(grid_rows, grid_cols, half_width).transpose(1, 0, 2)
    row_exit = carried_in(local_return(query_rows, row_prep, row_up), "gcol", chain_link, row_zero)[
        1
    ]
    parts_up, parts_query = (
        lax.all_gather(
            shortened(grad_mixed[:, half_width:].reshape(grid_rows, grid_cols, half_width)),
            "grow",
            axis=0,
            tiled=True,
        ),
        lax.all_gather(
            proj_bf[:, offset + 3 * state_size : offset + 4 * state_size].reshape(
                grid_rows, grid_cols, state_size
            ),
            "grow",
            axis=0,
            tiled=True,
        ),
    )
    col_exit = col_zero[1]
    for block_idx in reversed(range(grow_size)):
        lower_row = block_idx * grid_rows
        piece_up = parts_up[lower_row : lower_row + grid_rows].transpose(1, 0, 2)
        piece_queries = (
            parts_query[lower_row : lower_row + grid_rows].astype(jnp.float32).transpose(1, 0, 2)
        )
        piece_log = parts_log[lower_row : lower_row + grid_rows].transpose(1, 2, 0)
        whole_log, piece_back = local_return(piece_queries, prepare(piece_log), piece_up)
        moved = carry_on(whole_log, col_exit) + piece_back
        col_exit = jnp.where(block_idx > my_block, moved, col_exit)
    grad_row_in, grad_row_key, grad_row_query = local_grads(
        row_inputs, key_rows, query_rows, row_prep, row_entry, row_exit, row_up
    )
    grad_col_in, grad_col_key, grad_col_query = local_grads(
        col_inputs, key_cols, query_cols, col_prep, col_entry, col_exit, col_up
    )
    grad_values = jnp.concatenate(
        [
            grad_row_in.reshape(tok_count, half_width),
            grad_col_in.transpose(1, 0, 2).reshape(tok_count, half_width),
        ],
        axis=1,
    )
    grad_proj = jnp.concatenate(
        [
            grad_values * silu_grad(pre_values),
            grad_gate,
            grad_row_key.reshape(tok_count, state_size),
            grad_row_query.reshape(tok_count, state_size),
            grad_col_key.transpose(1, 0, 2).reshape(tok_count, state_size),
            grad_col_query.transpose(1, 0, 2).reshape(tok_count, state_size),
        ],
        axis=1,
    ).astype(jnp.bfloat16)
    keep_mask = present * (1 - masked).astype(jnp.bfloat16)[:, :, None]
    grad_model_in = jnp.dot(grad_proj, full_in, preferred_element_type=jnp.float32).reshape(
        grid_rows, grid_cols, feat_width
    )
    patch_grad = (grad_model_in * keep_mask).astype(jnp.bfloat16)
    return (patch_grad, out_weight_grad)


MESH = pl.DeviceIdType.MESH
NT = (((1,), (1,)), ((), ()))
NN = (((1,), (0,)), ((), ()))
TN = (((0,), (0,)), ((), ()))


def mm(a, b, dims):
    return lax.dot_general(a, b, dims, preferred_element_type=jnp.float32)


def group_barrier(chips, cores):
    me = lax.axis_index("gcol") * cores + lax.axis_index("grow")
    total = chips * cores
    barrier = pltpu.get_barrier_semaphore()
    for d in range(1, total):
        to = lax.rem(me + d, total)
        pl.semaphore_signal(
            barrier,
            inc=1,
            device_id={"gcol": to // cores, "grow": lax.rem(to, cores)},
            device_id_type=MESH,
        )
    pl.semaphore_wait(barrier, total - 1)


def scatter_kernel(
    chips, rows, tok_ref, rdec_ref, cdec_ref, w_ref, xg_ref, dec_ref, wo_ref,
    tok_send, tok_recv, dec_send, dec_recv, w_sem, loc_sem,
):
    k, c = lax.axis_index("gcol"), lax.axis_index("grow")
    group_barrier(chips, 2)

    def remote(src, dst, s, r, chip, core):
        return pltpu.make_async_remote_copy(
            src_ref=src, dst_ref=dst, send_sem=s, recv_sem=r,
            device_id={"gcol": chip, "grow": core}, device_id_type=MESH,
        )

    def row_pair(i):
        row = rows * c + i
        return (
            remote(tok_ref.at[i], xg_ref.at[k], tok_send.at[i], tok_recv.at[k], row, 0),
            remote(rdec_ref.at[i], dec_ref.at[k], dec_send.at[i], dec_recv.at[k], row, 0),
        )

    def row_local(i):
        return (
            pltpu.make_async_copy(tok_ref.at[i], xg_ref.at[k], loc_sem.at[0]),
            pltpu.make_async_copy(rdec_ref.at[i], dec_ref.at[k], loc_sem.at[1]),
        )

    def col_pair():
        lo = pl.ds(0, rows)
        return (
            remote(tok_ref, xg_ref.at[lo], tok_send.at[rows], tok_recv.at[chips], k, 1),
            remote(cdec_ref, dec_ref.at[lo], dec_send.at[rows], dec_recv.at[chips], k, 1),
        )

    def col_local():
        hi = pl.ds(rows, rows)
        return (
            pltpu.make_async_copy(tok_ref, xg_ref.at[hi], loc_sem.at[0]),
            pltpu.make_async_copy(cdec_ref, dec_ref.at[hi], loc_sem.at[1]),
        )

    weights = remote(w_ref, wo_ref, w_sem.at[0], w_sem.at[1], k, 1 - c)
    for i in range(rows):
        mine = jnp.logical_and(c == 0, k == i)

        @pl.when(jnp.logical_not(mine))
        def _():
            for copy in row_pair(i):
                copy.start()

        @pl.when(mine)
        def _():
            for copy in row_local(i):
                copy.start()

    @pl.when(c == 0)
    def _():
        for copy in col_pair():
            copy.start()

    @pl.when(c == 1)
    def _():
        for copy in col_local():
            copy.start()

    weights.start()

    for i in range(rows):
        mine = jnp.logical_and(c == 0, k == i)

        @pl.when(jnp.logical_not(mine))
        def _():
            for copy in row_pair(i):
                copy.wait_send()

        @pl.when(mine)
        def _():
            for copy in row_local(i):
                copy.wait()

    @pl.when(c == 0)
    def _():
        for copy in col_pair():
            copy.wait_send()
        for d in range(1, chips):
            src = lax.rem(k + d, chips)
            remote(tok_ref.at[0], xg_ref.at[src], tok_send.at[0], tok_recv.at[src], k, 1).wait_recv()
            remote(rdec_ref.at[0], dec_ref.at[src], dec_send.at[0], dec_recv.at[src], k, 1).wait_recv()

        @pl.when(k >= rows)
        def _():
            remote(tok_ref.at[0], xg_ref.at[k], tok_send.at[0], tok_recv.at[k], k, 1).wait_recv()
            remote(rdec_ref.at[0], dec_ref.at[k], dec_send.at[0], dec_recv.at[k], k, 1).wait_recv()

    @pl.when(c == 1)
    def _():
        for copy in col_local():
            copy.wait()
        lo = pl.ds(0, rows)
        remote(tok_ref, xg_ref.at[lo], tok_send.at[0], tok_recv.at[chips], k, 0).wait_recv()
        remote(cdec_ref, dec_ref.at[lo], dec_send.at[0], dec_recv.at[chips], k, 0).wait_recv()

    weights.wait()


def any_specs(count):
    return [pl.BlockSpec(memory_space=pl.ANY)] * count


def vmem_specs(count):
    return [pl.BlockSpec(memory_space=pltpu.VMEM)] * count


def distribute(chips, rows, tok, rdec, cdec, w):
    dma = pltpu.SemaphoreType.DMA
    return pl.pallas_call(
        functools.partial(scatter_kernel, chips, rows),
        name="distribute",
        out_shape=(
            jax.ShapeDtypeStruct((chips,) + tok.shape[1:], tok.dtype),
            jax.ShapeDtypeStruct((chips,) + rdec.shape[1:], rdec.dtype),
            jax.ShapeDtypeStruct(w.shape, w.dtype),
        ),
        in_specs=any_specs(4),
        out_specs=tuple(any_specs(3)),
        scratch_shapes=[
            dma((rows + 1,)), dma((chips + 1,)), dma((rows + 1,)), dma((chips + 1,)), dma((2,)), dma((2,)),
        ],
        compiler_params=pltpu.CompilerParams(collective_id=0, has_side_effects=True),
    )(tok, rdec, cdec, w)


def mixer_kernel(stride, xg_ref, dec_ref, wa_ref, wb_ref, wout_ref, gp_ref, wg_ref):
    c = lax.axis_index("grow")
    toks = xg_ref.shape[0]
    half, feat = wout_ref.shape[1], wout_ref.shape[0]
    part = wa_ref.shape[1]
    own = xg_ref[:, pl.ds(pl.multiple_of(c * part, part), part)]
    oth = xg_ref[:, pl.ds(pl.multiple_of((1 - c) * part, part), part)]

    def project(start, size):
        sel = pl.ds(pl.multiple_of(start, 128), size)
        acc = mm(own, wa_ref[sel, :], NT) + mm(oth, wb_ref[sel, :], NT)
        return acc.astype(jnp.bfloat16)

    u_bf = project(c * half, half)
    z_bf = project(2 * half + c * half, half)
    bc = project(4 * half + c * 2 * N, 2 * N)
    b_bf, c_bf = bc[:, :N], bc[:, N:]
    grads = xg_ref[:, feat:]
    gn_bf = mm(grads, wout_ref[...], NN).astype(jnp.bfloat16)

    t_at = lax.broadcasted_iota(jnp.int32, (toks, toks), 0)
    k_at = lax.broadcasted_iota(jnp.int32, (toks, toks), 1)
    step = jnp.where(c == 0, 1, stride)
    mask = jnp.logical_and(t_at >= k_at, lax.rem(t_at, step) == lax.rem(k_at, step))
    ones = mask.astype(jnp.float32)
    dec = dec_ref[...]
    run_s = lax.dot_general(ones, dec, NT, precision=PRECISE, preferred_element_type=jnp.float32)
    run_l = lax.dot_general(dec, ones, NT, precision=PRECISE, preferred_element_type=jnp.float32)
    scores = jnp.where(mask, mm(c_bf, b_bf, NT), 0.0)
    d_scores = jnp.zeros((toks, toks), jnp.float32)
    low = lax.broadcasted_iota(jnp.int32, (toks, 128), 1) < N

    def per_head(x):
        first = jnp.sum(jnp.where(low, x, 0.0), axis=1, keepdims=True)
        second = jnp.sum(jnp.where(low, 0.0, x), axis=1, keepdims=True)
        return jnp.where(low, first, second) * (1.0 / N)

    for p in range(half // 128):
        cols = slice(p * 128, (p + 1) * 128)
        u = u_bf[:, cols].astype(jnp.float32)
        z = z_bf[:, cols].astype(jnp.float32)
        sig_u = 1.0 / (1.0 + jnp.exp(-u))
        sig_z = 1.0 / (1.0 + jnp.exp(-z))
        val_bf = (u * sig_u).astype(jnp.bfloat16)
        decays, mats = [], []
        for h in (2 * p, 2 * p + 1):
            gap = run_s[:, h : h + 1] - run_l[h : h + 1, :]
            decay = jnp.exp(jnp.minimum(gap, 0.0))
            decays.append(decay)
            mats.append((decay * scores).astype(jnp.bfloat16))
        y = jnp.where(low, mm(mats[0], val_bf, NN), mm(mats[1], val_bf, NN))
        gate = z * sig_z
        gated = y * gate
        inv = lax.rsqrt(per_head(gated * gated) + EPSILON)
        normed = gated * inv
        wg_ref[:, cols] = mm(grads, normed.astype(jnp.bfloat16), TN).astype(wg_ref.dtype)
        gn = gn_bf[:, cols].astype(jnp.float32)
        gg = inv * (gn - normed * per_head(gn * normed))
        dy = gg * gate
        dz = gg * y * (sig_z * (1.0 + z * (1.0 - sig_z)))
        gp_ref[:, half + p * 128 : half + (p + 1) * 128] = dz.astype(jnp.bfloat16)
        dy_bf = dy.astype(jnp.bfloat16)
        dv = jnp.where(low, mm(mats[0], dy_bf, TN), mm(mats[1], dy_bf, TN))
        du = dv * (sig_u * (1.0 + u * (1.0 - sig_u)))
        gp_ref[:, cols] = du.astype(jnp.bfloat16)
        zero = jnp.zeros_like(dy)
        d_scores += decays[0] * mm(jnp.where(low, dy, zero).astype(jnp.bfloat16), val_bf, NT)
        d_scores += decays[1] * mm(jnp.where(low, zero, dy).astype(jnp.bfloat16), val_bf, NT)

    ds_bf = jnp.where(mask, d_scores, 0.0).astype(jnp.bfloat16)
    d_key = mm(ds_bf, c_bf, TN)
    d_query = mm(ds_bf, b_bf, NN)
    gp_ref[:, 2 * half :] = jnp.concatenate([d_key, d_query], axis=1).astype(jnp.bfloat16)


def mixer(stride, xg, dec, wa, wb, wout):
    toks, half, feat = xg.shape[0], wout.shape[1], wout.shape[0]
    return pl.pallas_call(
        functools.partial(mixer_kernel, stride),
        name="mixer",
        out_shape=(
            jax.ShapeDtypeStruct((toks, 2 * half + 2 * N), jnp.bfloat16),
            jax.ShapeDtypeStruct((feat, half), jnp.bfloat16),
        ),
        in_specs=vmem_specs(5),
        out_specs=tuple(vmem_specs(2)),
        compiler_params=pltpu.CompilerParams(vmem_limit_bytes=48 << 20),
    )(xg, dec, wa, wb, wout)


def gather_kernel(
    chips, rows, gp_ref, wg_ref, row_ref, col_ref, sum_ref,
    gp_send, gp_recv, wg_send, wg_recv, loc_sem,
):
    k, c = lax.axis_index("gcol"), lax.axis_index("grow")
    total = 2 * chips
    me = 2 * k + c
    group_barrier(chips, 2)

    def remote(src, dst, s, r, chip, core):
        return pltpu.make_async_remote_copy(
            src_ref=src, dst_ref=dst, send_sem=s, recv_sem=r,
            device_id={"gcol": chip, "grow": core}, device_id_type=MESH,
        )

    home_core = k // rows
    slot = lax.rem(k, rows)

    def row_back(chip):
        return remote(
            gp_ref.at[chip], row_ref.at[slot], gp_send.at[chip], gp_recv.at[slot], chip, home_core
        )

    def row_local():
        return pltpu.make_async_copy(gp_ref.at[k], row_ref.at[slot], loc_sem.at[0])

    def col_back():
        return remote(gp_ref.at[pl.ds(0, rows)], col_ref, gp_send.at[chips], gp_recv.at[rows], k, 0)

    def col_local():
        return pltpu.make_async_copy(gp_ref.at[pl.ds(rows, rows)], col_ref, loc_sem.at[0])

    def spread(to):
        return remote(
            wg_ref.at[to], sum_ref.at[me], wg_send.at[to], wg_recv.at[me], to // 2, lax.rem(to, 2)
        )

    own_sum = pltpu.make_async_copy(wg_ref.at[me], sum_ref.at[me], loc_sem.at[1])
    own_sum.start()

    @pl.when(c == 0)
    def _():
        for d in range(1, chips):
            row_back(lax.rem(k + d, chips)).start()

        @pl.when(home_core == 0)
        def _():
            row_local().start()

        @pl.when(home_core == 1)
        def _():
            row_back(k).start()

    @pl.when(c == 1)
    def _():
        col_back().start()
        col_local().start()

    for d in range(1, total):
        spread(lax.rem(me + d, total)).start()

    own_sum.wait()

    @pl.when(c == 0)
    def _():
        for d in range(1, chips):
            row_back(lax.rem(k + d, chips)).wait_send()

        @pl.when(home_core == 0)
        def _():
            row_local().wait()

        @pl.when(home_core == 1)
        def _():
            row_back(k).wait_send()

        remote(gp_ref.at[pl.ds(0, rows)], col_ref, gp_send.at[chips], gp_recv.at[rows], k, 1).wait_recv()

    @pl.when(c == 1)
    def _():
        col_back().wait_send()
        col_local().wait()

    for i in range(rows):
        mine = jnp.logical_and(c == 0, k == i)

        @pl.when(jnp.logical_not(mine))
        def _():
            remote(gp_ref.at[0], row_ref.at[i], gp_send.at[0], gp_recv.at[i], k, 1 - c).wait_recv()

    for d in range(1, total):
        to = lax.rem(me + d, total)
        spread(to).wait_send()
        remote(wg_ref.at[0], sum_ref.at[to], wg_send.at[0], wg_recv.at[to], k, 1 - c).wait_recv()


def bring_home(chips, rows, gp, wg):
    dma = pltpu.SemaphoreType.DMA
    back = jax.ShapeDtypeStruct((rows,) + gp.shape[1:], gp.dtype)
    return pl.pallas_call(
        functools.partial(gather_kernel, chips, rows),
        name="bring_home",
        out_shape=(back, back, jax.ShapeDtypeStruct(wg.shape, wg.dtype)),
        in_specs=any_specs(2),
        out_specs=tuple(any_specs(3)),
        scratch_shapes=[
            dma((chips + 1,)), dma((rows + 1,)), dma((2 * chips,)), dma((2 * chips,)), dma((2,)),
        ],
        compiler_params=pltpu.CompilerParams(collective_id=1, has_side_effects=True),
    )(gp, wg)


def finish_kernel(scale, row_ref, col_ref, sum_ref, keep_ref, wa_ref, wb_ref, pg_ref, out_ref):
    c = lax.axis_index("grow")
    part = wa_ref.shape[1]
    half = (row_ref.shape[1] - 2 * N) // 2
    keep = keep_ref[...]
    for w_ref, side in ((wa_ref, c), (wb_ref, 1 - c)):
        acc = jnp.zeros((row_ref.shape[0], part), jnp.float32)
        for g, gp_ref in enumerate((row_ref, col_ref)):
            acc += mm(gp_ref[:, :half], w_ref[g * half : (g + 1) * half, :], NN)
            acc += mm(gp_ref[:, half : 2 * half], w_ref[(2 + g) * half : (3 + g) * half, :], NN)
            at = 4 * half + g * 2 * N
            acc += mm(gp_ref[:, 2 * half :], w_ref[at : at + 2 * N, :], NN)
        pg_ref[:, pl.ds(pl.multiple_of(side * part, part), part)] = (acc * keep).astype(pg_ref.dtype)
    width = sum_ref.shape[2]
    for core in range(2):
        acc = sum_ref[core].astype(jnp.float32)
        for chip in range(1, sum_ref.shape[0] // 2):
            acc += sum_ref[2 * chip + core].astype(jnp.float32)
        out_ref[:, core * width : (core + 1) * width] = acc * scale


def finish(scale, row, col, sums, keep, wa, wb):
    return pl.pallas_call(
        functools.partial(finish_kernel, scale),
        name="finish",
        out_shape=(
            jax.ShapeDtypeStruct((row.shape[0], 2 * wa.shape[1]), jnp.bfloat16),
            jax.ShapeDtypeStruct((sums.shape[1], 2 * sums.shape[2]), jnp.float32),
        ),
        in_specs=vmem_specs(6),
        out_specs=tuple(vmem_specs(2)),
        compiler_params=pltpu.CompilerParams(vmem_limit_bytes=48 << 20),
    )(row, col, sums, keep, wa, wb)


def owned(
    patches, mask_token, masked, tissue, in_weight, out_weight, row_decay, col_decay, cotangent
):
    rows, cols, feat = patches.shape
    chips = lax.axis_size("gcol")
    present = tissue.astype(jnp.bfloat16)[:, :, None]
    hidden = masked.astype(jnp.bfloat16)[:, :, None]
    model_in = jnp.where((masked == 1)[:, :, None], mask_token[None, None, :], patches) * present
    tok = jnp.concatenate([model_in, cotangent * hidden], axis=2)
    xg, dec, other = distribute(
        chips, rows, tok, row_decay.transpose(1, 0, 2), col_decay.transpose(1, 0, 2), in_weight
    )
    toks = chips * cols
    gp, wg = mixer(
        cols,
        xg.reshape(toks, 2 * feat),
        dec.transpose(1, 0, 2).reshape(-1, toks),
        in_weight,
        other,
        out_weight,
    )
    row, col, sums = bring_home(
        chips, rows, gp.reshape(chips, cols, -1), wg.reshape(2 * chips, -1, wg.shape[1])
    )
    keep = (tissue * (1 - masked)).astype(jnp.float32).reshape(rows * cols, 1)
    scale = 1.0 / math.sqrt(2 * rows * cols * chips)
    pg, out = finish(
        scale,
        row.reshape(rows * cols, -1),
        col.reshape(rows * cols, -1),
        sums,
        keep,
        in_weight,
        other,
    )
    return pg.reshape(rows, cols, feat), out


def body(*args):
    rows = args[0].shape[0]
    if lax.axis_size("grow") == 2 and lax.axis_size("gcol") == 2 * rows:
        return owned(*args)
    return shards(*args)


def solution(mesh):
    return jax.shard_map(
        body,
        mesh=mesh,
        in_specs=(
            P(("groups", "grow"), "gcol", None),
            P(),
            P(("groups", "grow"), "gcol"),
            P(("groups", "grow"), "gcol"),
            P(None, "grow"),
            P(None, "grow"),
            P(None, ("groups", "grow"), "gcol"),
            P(None, ("groups", "grow"), "gcol"),
            P(("groups", "grow"), "gcol", None),
        ),
        out_specs=(P(("groups", "grow"), "gcol", None), P(("groups", "gcol", "grow"), None)),
        check_vma=False,
    )
```

```python
import functools
import math

import jax
import jax.numpy as jnp
from jax import lax
from jax.experimental import pallas as pl
from jax.experimental.pallas import tpu as pltpu
from jax.sharding import PartitionSpec as P

E = 1024
HEADS = 16
N = 64


EPSILON = 1e-05
PRECISE = lax.Precision.HIGHEST


def prefix(value, axis, join, neutral):
    count, mine = (lax.axis_size(axis), lax.axis_index(axis))
    pieces = jax.tree.map(lambda part: lax.all_gather(part, axis), value)
    so_far = jax.tree.map(
        lambda part, zero: jnp.full_like(part, 0) + jnp.asarray(zero, part.dtype), value, neutral
    )

    def prefix_hop(position, so_far):
        longer = join(so_far, jax.tree.map(lambda part: part[position], pieces))
        return jax.tree.map(lambda new, old: jnp.where(position < mine, new, old), longer, so_far)

    return lax.fori_loop(0, count - 1, prefix_hop, so_far)


def carried_in(shard, axis, combine, identity):
    length, position = (lax.axis_size(axis), lax.axis_index(axis))
    everything = jax.tree.map(
        lambda part, kind: lax.all_gather(part.astype(kind), axis),
        shard,
        jax.tree.map(lambda a: jnp.bfloat16 if a.dtype == jnp.float32 else a.dtype, shard),
    )
    start = jax.tree.map(
        lambda part, zero: jnp.broadcast_to(jnp.asarray(zero, part.dtype), part.shape),
        shard,
        identity,
    )

    def carried_hop(k, before):
        at = length - 1 - k
        reached = at > position
        new = combine(
            before, jax.tree.map(lambda part, own: part[at].astype(own.dtype), everything, shard)
        )
        return jax.tree.map(lambda a, b: jnp.where(reached, a, b), new, before)

    return lax.fori_loop(0, length, carried_hop, start)


def shortened(shard):

    def short(part):
        return part.astype(jnp.bfloat16) if part.dtype == jnp.float32 else part

    return jax.tree.map(short, shard)


def silu_grad(pre_act):
    sigmoid_v = jax.nn.sigmoid(pre_act)
    return sigmoid_v * (1.0 + pre_act * (1.0 - sigmoid_v))


def per_channel(head_part, channels):
    return jnp.repeat(head_part, channels // head_part.shape[-1], axis=-1)


def line_form(head_lines, channels):
    return per_channel(head_lines.transpose(1, 2, 0), channels)


def carry_on(log_lines, state):
    return per_channel(jnp.exp(log_lines), state.shape[2])[:, None, :] * state


def prepare(log_decay):
    length = log_decay.shape[2]
    running = jnp.cumsum(log_decay, axis=2)
    whole_log = running[:, :, -1]
    causal = jnp.arange(length)[:, None] >= jnp.arange(length)[None, :]
    log_gaps = running[:, :, :, None] - running[:, :, None, :]
    decay_mat = jnp.where(causal, jnp.exp(jnp.where(causal, log_gaps, 0.0)), 0.0)
    return (running, whole_log, decay_mat)


def chain_link(earlier, later):
    return (earlier[0] + later[0], carry_on(later[0], earlier[1]) + later[1])


def split_heads(lines, head_count):
    line_count, length, channels = lines.shape
    return lines.reshape(line_count, length, head_count, channels // head_count)


def local_summary(inputs, key_vecs, prepared):
    running, whole_log, decay_mat = prepared
    to_end = line_form(jnp.exp(whole_log[:, :, None] - running), inputs.shape[2])
    fresh = jnp.einsum("ltc,ltn->lnc", inputs * to_end, key_vecs, precision=PRECISE)
    return (whole_log.T, fresh)


def local_return(query_vecs, prepared, upstream):
    running, whole_log, decay_mat = prepared
    from_start = line_form(jnp.exp(running), upstream.shape[2])
    backward = jnp.einsum("ltc,ltn->lnc", upstream * from_start, query_vecs, precision=PRECISE)
    return (whole_log.T, backward)


def local_outputs(inputs, key_vecs, query_vecs, prepared, incoming):
    running, whole_log, decay_mat = prepared
    head_count = decay_mat.shape[0]
    line_count, length, channels = inputs.shape
    scores = jnp.einsum("ltn,lkn->ltk", query_vecs, key_vecs, precision=PRECISE)
    within = jnp.einsum(
        "gltk,lkgp->ltgp",
        decay_mat * scores[None],
        split_heads(inputs, head_count),
        precision=PRECISE,
    )
    within = within.reshape(line_count, length, channels)
    carried = jnp.einsum("ltn,lnc->ltc", query_vecs, incoming, precision=PRECISE)
    return within + carried * line_form(jnp.exp(running), channels)


def local_grads(inputs, key_vecs, query_vecs, prepared, incoming, returning, upstream):
    running, whole_log, decay_mat = prepared
    head_count = decay_mat.shape[0]
    line_count, length, channels = inputs.shape
    from_start = line_form(jnp.exp(running), channels)
    to_end = line_form(jnp.exp(whole_log[:, :, None] - running), channels)
    scores = jnp.einsum("ltn,lkn->ltk", query_vecs, key_vecs, precision=PRECISE)
    heads_up = split_heads(upstream, head_count)
    heads_in = split_heads(inputs, head_count)
    grad_inputs = jnp.einsum(
        "gltk,ltgp->lkgp", decay_mat * scores[None], heads_up, precision=PRECISE
    ).reshape(line_count, length, channels)
    grad_inputs = (
        grad_inputs + jnp.einsum("lnc,lkn->lkc", returning, key_vecs, precision=PRECISE) * to_end
    )
    mixed = jnp.einsum("ltgp,lkgp->gltk", heads_up, heads_in, precision=PRECISE) * decay_mat
    grad_keys = jnp.einsum("gltk,ltn->lkn", mixed, query_vecs, precision=PRECISE)
    grad_keys = grad_keys + jnp.einsum(
        "lkc,lnc->lkn", inputs * to_end, returning, precision=PRECISE
    )
    grad_queries = jnp.einsum("gltk,lkn->ltn", mixed, key_vecs, precision=PRECISE)
    grad_queries = grad_queries + jnp.einsum(
        "ltc,lnc->ltn", upstream * from_start, incoming, precision=PRECISE
    )
    return (grad_inputs, grad_keys, grad_queries)


def shards(
    patches, mask_token, masked, tissue, in_weight, out_weight, row_decay, col_decay, cotangent
):
    grid_rows, grid_cols, feat_width = patches.shape
    tok_count = grid_rows * grid_cols
    chosen = (masked == 1)[:, :, None]
    present = tissue.astype(jnp.bfloat16)[:, :, None]
    model_in = jnp.where(chosen, mask_token[None, None, :], patches) * present
    flat_in = model_in.reshape(tok_count, feat_width)
    inner_width = E
    half_width = inner_width // 2
    state_size = N
    number_of_heads = HEADS // 2
    offset = 2 * inner_width
    full_in, full_out = (
        lax.all_gather(in_weight, "grow", axis=1, tiled=True),
        lax.all_gather(out_weight, "grow", axis=1, tiled=True),
    )
    projected = lax.dot_general(
        flat_in, full_in, (((1,), (1,)), ((), ())), preferred_element_type=jnp.float32
    )
    proj_bf = projected.astype(jnp.bfloat16)
    pre_values = proj_bf[:, :inner_width].astype(jnp.float32)
    gate_pre = proj_bf[:, inner_width:offset].astype(jnp.float32)
    key_rows = (
        proj_bf[:, offset : offset + state_size]
        .astype(jnp.float32)
        .reshape(grid_rows, grid_cols, state_size)
    )
    query_rows = (
        proj_bf[:, offset + state_size : offset + 2 * state_size]
        .astype(jnp.float32)
        .reshape(grid_rows, grid_cols, state_size)
    )
    key_cols = (
        proj_bf[:, offset + 2 * state_size : offset + 3 * state_size]
        .astype(jnp.float32)
        .reshape(grid_rows, grid_cols, state_size)
        .transpose(1, 0, 2)
    )
    query_cols = (
        proj_bf[:, offset + 3 * state_size : offset + 4 * state_size]
        .astype(jnp.float32)
        .reshape(grid_rows, grid_cols, state_size)
        .transpose(1, 0, 2)
    )
    values = jax.nn.silu(pre_values)
    row_inputs = values[:, :half_width].reshape(grid_rows, grid_cols, half_width)
    col_inputs = values[:, half_width:].reshape(grid_rows, grid_cols, half_width).transpose(1, 0, 2)
    row_prep = prepare(row_decay)
    col_prep = prepare(col_decay.transpose(0, 2, 1))
    row_zero = (
        jnp.zeros((grid_rows, number_of_heads), jnp.float32),
        jnp.zeros((grid_rows, state_size, half_width), jnp.float32),
    )
    col_zero = (
        jnp.zeros((grid_cols, number_of_heads), jnp.float32),
        jnp.zeros((grid_cols, state_size, half_width), jnp.float32),
    )
    row_entry = prefix(local_summary(row_inputs, key_rows, row_prep), "gcol", chain_link, row_zero)[
        1
    ]
    grow_size = lax.axis_size("grow")
    my_block = lax.axis_index("grow")
    parts_in, parts_key, parts_log = (
        lax.all_gather(
            proj_bf[:, half_width:inner_width].reshape(grid_rows, grid_cols, half_width),
            "grow",
            axis=0,
            tiled=True,
        ),
        lax.all_gather(
            proj_bf[:, offset + 2 * state_size : offset + 3 * state_size].reshape(
                grid_rows, grid_cols, state_size
            ),
            "grow",
            axis=0,
            tiled=True,
        ),
        lax.all_gather(
            col_decay.transpose(1, 0, 2).astype(jnp.bfloat16), "grow", axis=0, tiled=True
        ).astype(jnp.float32),
    )
    col_entry = col_zero[1]
    for block_idx in range(grow_size):
        lower_row = block_idx * grid_rows
        piece_in = jax.nn.silu(
            parts_in[lower_row : lower_row + grid_rows].astype(jnp.float32)
        ).transpose(1, 0, 2)
        piece_keys = (
            parts_key[lower_row : lower_row + grid_rows].astype(jnp.float32).transpose(1, 0, 2)
        )
        piece_log = parts_log[lower_row : lower_row + grid_rows].transpose(1, 2, 0)
        whole_log, piece_state = local_summary(piece_in, piece_keys, prepare(piece_log))
        moved = carry_on(whole_log, col_entry) + piece_state
        col_entry = jnp.where(block_idx < my_block, moved, col_entry)
    row_out = local_outputs(row_inputs, key_rows, query_rows, row_prep, row_entry)
    col_out = local_outputs(col_inputs, key_cols, query_cols, col_prep, col_entry).transpose(
        1, 0, 2
    )
    mixed = jnp.concatenate(
        [row_out.reshape(tok_count, half_width), col_out.reshape(tok_count, half_width)], axis=1
    )
    gate_act = jax.nn.silu(gate_pre)
    head_size = inner_width // HEADS
    gated = (mixed * gate_act).reshape(tok_count, HEADS, head_size)
    inv_rms = lax.rsqrt(jnp.mean(gated * gated, axis=2, keepdims=True) + EPSILON)
    normed = gated * inv_rms
    normed_bf = normed.reshape(tok_count, inner_width).astype(jnp.bfloat16)
    grad_out = (cotangent * masked.astype(jnp.bfloat16)[:, :, None]).reshape(tok_count, feat_width)
    total_patches = tok_count * lax.axis_size("gcol") * lax.axis_size("grow")
    weight_sum = lax.psum_scatter(
        lax.dot_general(
            grad_out, normed_bf, (((0,), (0,)), ((), ())), preferred_element_type=jnp.float32
        ),
        ("gcol", "grow"),
        scatter_dimension=0,
        tiled=True,
    )
    out_weight_grad = weight_sum * (1.0 / math.sqrt(total_patches))
    grad_normed_bf = jnp.dot(grad_out, full_out, preferred_element_type=jnp.float32).astype(
        jnp.bfloat16
    )
    grad_normed = lax.optimization_barrier(grad_normed_bf).astype(jnp.float32)
    grad_normed = grad_normed.reshape(tok_count, HEADS, head_size)
    grad_gated = inv_rms * (
        grad_normed - normed * jnp.mean(grad_normed * normed, axis=2, keepdims=True)
    )
    grad_gated = grad_gated.reshape(tok_count, inner_width)
    grad_mixed = grad_gated * gate_act
    grad_gate = grad_gated * mixed * silu_grad(gate_pre)
    row_up = grad_mixed[:, :half_width].reshape(grid_rows, grid_cols, half_width)
    col_up = grad_mixed[:, half_width:].reshape(grid_rows, grid_cols, half_width).transpose(1, 0, 2)
    row_exit = carried_in(local_return(query_rows, row_prep, row_up), "gcol", chain_link, row_zero)[
        1
    ]
    parts_up, parts_query = (
        lax.all_gather(
            shortened(grad_mixed[:, half_width:].reshape(grid_rows, grid_cols, half_width)),
            "grow",
            axis=0,
            tiled=True,
        ),
        lax.all_gather(
            proj_bf[:, offset + 3 * state_size : offset + 4 * state_size].reshape(
                grid_rows, grid_cols, state_size
            ),
            "grow",
            axis=0,
            tiled=True,
        ),
    )
    col_exit = col_zero[1]
    for block_idx in reversed(range(grow_size)):
        lower_row = block_idx * grid_rows
        piece_up = parts_up[lower_row : lower_row + grid_rows].transpose(1, 0, 2)
        piece_queries = (
            parts_query[lower_row : lower_row + grid_rows].astype(jnp.float32).transpose(1, 0, 2)
        )
        piece_log = parts_log[lower_row : lower_row + grid_rows].transpose(1, 2, 0)
        whole_log, piece_back = local_return(piece_queries, prepare(piece_log), piece_up)
        moved = carry_on(whole_log, col_exit) + piece_back
        col_exit = jnp.where(block_idx > my_block, moved, col_exit)
    grad_row_in, grad_row_key, grad_row_query = local_grads(
        row_inputs, key_rows, query_rows, row_prep, row_entry, row_exit, row_up
    )
    grad_col_in, grad_col_key, grad_col_query = local_grads(
        col_inputs, key_cols, query_cols, col_prep, col_entry, col_exit, col_up
    )
    grad_values = jnp.concatenate(
        [
            grad_row_in.reshape(tok_count, half_width),
            grad_col_in.transpose(1, 0, 2).reshape(tok_count, half_width),
        ],
        axis=1,
    )
    grad_proj = jnp.concatenate(
        [
            grad_values * silu_grad(pre_values),
            grad_gate,
            grad_row_key.reshape(tok_count, state_size),
            grad_row_query.reshape(tok_count, state_size),
            grad_col_key.transpose(1, 0, 2).reshape(tok_count, state_size),
            grad_col_query.transpose(1, 0, 2).reshape(tok_count, state_size),
        ],
        axis=1,
    ).astype(jnp.bfloat16)
    keep_mask = present * (1 - masked).astype(jnp.bfloat16)[:, :, None]
    grad_model_in = jnp.dot(grad_proj, full_in, preferred_element_type=jnp.float32).reshape(
        grid_rows, grid_cols, feat_width
    )
    patch_grad = (grad_model_in * keep_mask).astype(jnp.bfloat16)
    return (patch_grad, out_weight_grad)


MESH = pl.DeviceIdType.MESH
NT = (((1,), (1,)), ((), ()))
NN = (((1,), (0,)), ((), ()))
TN = (((0,), (0,)), ((), ()))


def mm(a, b, dims):
    return lax.dot_general(a, b, dims, preferred_element_type=jnp.float32)


def layer_kernel(
    chips, rows, scale,
    patch_ref, token_ref, cot_ref, flag_ref, rdec_ref, cdec_ref, w_hbm, wout_hbm,
    pg_ref, out_ref,
    xs, gs, rd, cd, xb, gb, db, wa, wb, wout, u_s, z_s, gn_s, bc_s, normed_s, y_s, mat_s, dec_s, gp, grow, gcol,
    xsend, wgo, xr, zs, zr,
    x_send, x_recv, g_send, g_recv, d_send, d_recv, w_sem, l_sem,
    gp_send, gp_recv, xr_send, xr_recv, z_send, z_recv,
):
    k, c = lax.axis_index("gcol"), lax.axis_index("grow")
    depth = chips // 2
    zi, xi = k // 2, lax.rem(k, 2)
    cols, feat = patch_ref.shape[1], patch_ref.shape[2]
    toks = chips * cols
    half, part = wout.shape[1], wa.shape[1]
    total = 2 * chips

    load_w = pltpu.make_async_copy(w_hbm, wa, l_sem.at[0])
    load_o = pltpu.make_async_copy(wout_hbm, wout, l_sem.at[1])
    load_w.start()
    load_o.start()

    me = 2 * k + c
    barrier = pltpu.get_barrier_semaphore()
    for d in range(1, total):
        to = lax.rem(me + d, total)
        pl.semaphore_signal(
            barrier, inc=1, device_id={"gcol": to // 2, "grow": lax.rem(to, 2)}, device_id_type=MESH
        )

    def remote(src, dst, s, r, chip, core):
        return pltpu.make_async_remote_copy(
            src_ref=src, dst_ref=dst, send_sem=s, recv_sem=r,
            device_id={"gcol": chip, "grow": core}, device_id_type=MESH,
        )

    for i in range(rows):
        flags = flag_ref[i]
        hidden, present = flags[:, 0:1], flags[:, 1:2]
        chosen = jnp.where(
            hidden > 0.5, token_ref[...].astype(jnp.float32), patch_ref[i].astype(jnp.float32)
        )
        xs[i] = (chosen * present).astype(jnp.bfloat16)
        gs[i] = (cot_ref[i].astype(jnp.float32) * hidden).astype(jnp.bfloat16)
        rd[i] = rdec_ref[:, i, :]
        cd[i] = cdec_ref[:, i, :]

    streams = (
        (xs, xs, xb, x_send, x_recv),
        (rd, cd, db, d_send, d_recv),
        (gs, gs, gb, g_send, g_recv),
    )

    def row_out(stream, i):
        row_src, _, dst, s, r = stream
        return remote(row_src.at[i], dst.at[k], s.at[i], r.at[k], rows * c + i, 0)

    def col_out(stream):
        _, col_src, dst, s, r = stream
        return remote(col_src, dst.at[pl.ds(0, rows)], s.at[rows], r.at[chips], k, 1)

    def row_in(stream, src):
        row_src, _, dst, s, r = stream
        return remote(row_src.at[0], dst.at[src], s.at[0], r.at[src], k, 1 - c)

    def col_in(stream):
        _, col_src, dst, s, r = stream
        return remote(col_src, dst.at[pl.ds(0, rows)], s.at[rows], r.at[chips], k, 1 - c)

    def launch(stream):
        for i in range(rows):

            @pl.when(jnp.logical_or(c == 1, k != i))
            def _():
                row_out(stream, i).start()

        @pl.when(c == 0)
        def _():
            col_out(stream).start()

    def arrive(stream):
        @pl.when(c == 0)
        def _():
            for d in range(1, chips):
                row_in(stream, lax.rem(k + d, chips)).wait_recv()

            @pl.when(k >= rows)
            def _():
                row_in(stream, k).wait_recv()

        @pl.when(c == 1)
        def _():
            col_in(stream).wait_recv()

    def drain(stream):
        for i in range(rows):

            @pl.when(jnp.logical_or(c == 1, k != i))
            def _():
                row_out(stream, i).wait_send()

        @pl.when(c == 0)
        def _():
            col_out(stream).wait_send()

    pl.semaphore_wait(barrier, total - 1)
    weights = remote(w_hbm, wb, w_sem.at[0], w_sem.at[1], k, 1 - c)
    launch(streams[0])
    launch(streams[1])
    weights.start()
    launch(streams[2])

    for row_src, col_src, dst, _, _ in streams:

        @pl.when(c == 1)
        def _():
            dst[pl.ds(rows, rows)] = col_src[...]

        for i in range(rows):

            @pl.when(jnp.logical_and(c == 0, k == i))
            def _():
                dst[i] = row_src[i]

    t_at = lax.broadcasted_iota(jnp.int32, (toks, toks), 0)
    k_at = lax.broadcasted_iota(jnp.int32, (toks, toks), 1)
    step = jnp.where(c == 0, 1, cols)
    mask = jnp.logical_and(t_at >= k_at, lax.rem(t_at, step) == lax.rem(k_at, step))
    low = lax.broadcasted_iota(jnp.int32, (toks, 128), 1) < N

    arrive(streams[1])
    ones = mask.astype(jnp.float32)
    dec = jnp.concatenate([db[i] for i in range(chips)], axis=1)
    run_s = lax.dot_general(ones, dec, NT, precision=PRECISE, preferred_element_type=jnp.float32)
    run_l = lax.dot_general(dec, ones, NT, precision=PRECISE, preferred_element_type=jnp.float32)
    heads = dec.shape[0]
    for h in range(heads):
        gap = run_s[:, h : h + 1] - run_l[h : h + 1, :]
        dec_s[h] = jnp.where(mask, jnp.exp(jnp.minimum(gap, 0.0)), 0.0)

    load_w.wait()
    arrive(streams[0])
    mine, rest = pl.multiple_of(c * part, part), pl.multiple_of((1 - c) * part, part)
    own = xb[:, :, pl.ds(mine, part)].reshape(toks, part)
    oth = xb[:, :, pl.ds(rest, part)].reshape(toks, part)
    pieces = ((u_s, c * half, half), (z_s, 2 * half + c * half, half), (bc_s, 4 * half + c * 2 * N, 2 * N))
    partial = [
        mm(own, wa[pl.ds(pl.multiple_of(start, 128), size), :], NT) for _, start, size in pieces
    ]
    weights.wait_recv()
    for (dst, start, size), first in zip(pieces, partial):
        second = mm(oth, wb[pl.ds(pl.multiple_of(start, 128), size), :], NT)
        dst[...] = (first + second).astype(jnp.bfloat16)

    b_bf, c_bf = bc_s[:, :N], bc_s[:, N:]
    scores = mm(c_bf, b_bf, NT)

    def per_head(x):
        first = jnp.sum(jnp.where(low, x, 0.0), axis=1, keepdims=True)
        second = jnp.sum(jnp.where(low, 0.0, x), axis=1, keepdims=True)
        return jnp.where(low, first, second) * (1.0 / N)

    def norm(p):
        cols_p = slice(p * 128, (p + 1) * 128)
        z = z_s[:, cols_p].astype(jnp.float32)
        sig_z = 1.0 / (1.0 + jnp.exp(-z))
        y = y_s[:, cols_p]
        gated = y * (z * sig_z)
        inv = lax.rsqrt(per_head(gated * gated) + EPSILON)
        return cols_p, z, sig_z, y, inv, gated * inv

    for p in range(half // 128):
        cols_p = slice(p * 128, (p + 1) * 128)
        u = u_s[:, cols_p].astype(jnp.float32)
        val_bf = (u / (1.0 + jnp.exp(-u))).astype(jnp.bfloat16)
        for h in (2 * p, 2 * p + 1):
            mat_s[h] = (dec_s[h] * scores).astype(jnp.bfloat16)
        y_s[:, cols_p] = jnp.where(
            low, mm(mat_s[2 * p], val_bf, NN), mm(mat_s[2 * p + 1], val_bf, NN)
        )
        normed_s[:, cols_p] = norm(p)[-1].astype(jnp.bfloat16)

    load_o.wait()
    arrive(streams[2])

    def weight_block(chip):
        at = pl.ds(pl.multiple_of(chip * 128, 128), 128)
        return mm(gb[:, :, at].reshape(toks, 128), normed_s[...], TN)

    def across(q):
        return remote(xsend.at[q], xr.at[q], xr_send.at[q], xr_recv.at[q], 2 * zi + 1 - xi, c)

    order = [lax.rem(zi + 1 + j, depth) for j in range(depth)]
    for q in order:
        xsend[q] = weight_block(2 * q + 1 - xi).astype(jnp.bfloat16)
        across(q).start()

    grads = gb[...].reshape(toks, feat)
    gn_s[...] = mm(grads, wout[...], NN).astype(jnp.bfloat16)
    d_scores = jnp.zeros((toks, toks), jnp.float32)
    for p in range(half // 128):
        cols_p, z, sig_z, y, inv, normed = norm(p)
        u = u_s[:, cols_p].astype(jnp.float32)
        sig_u = 1.0 / (1.0 + jnp.exp(-u))
        val_bf = (u * sig_u).astype(jnp.bfloat16)
        gn = gn_s[:, cols_p].astype(jnp.float32)
        gg = inv * (gn - normed * per_head(gn * normed))
        dy = gg * (z * sig_z)
        dz = gg * y * (sig_z * (1.0 + z * (1.0 - sig_z)))
        dy_bf = dy.astype(jnp.bfloat16)
        dv = jnp.where(low, mm(mat_s[2 * p], dy_bf, TN), mm(mat_s[2 * p + 1], dy_bf, TN))
        du = dv * (sig_u * (1.0 + u * (1.0 - sig_u)))
        gp[:, :, cols_p] = du.astype(jnp.bfloat16).reshape(chips, cols, 128)
        gp[:, :, half + p * 128 : half + (p + 1) * 128] = dz.astype(jnp.bfloat16).reshape(
            chips, cols, 128
        )
        zero = jnp.zeros_like(dy)
        d_scores += dec_s[2 * p] * mm(jnp.where(low, dy, zero).astype(jnp.bfloat16), val_bf, NT)
        d_scores += dec_s[2 * p + 1] * mm(jnp.where(low, zero, dy).astype(jnp.bfloat16), val_bf, NT)
    ds_bf = d_scores.astype(jnp.bfloat16)
    d_bc = jnp.concatenate([mm(ds_bf, c_bf, TN), mm(ds_bf, b_bf, NN)], axis=1)
    gp[:, :, 2 * half :] = d_bc.astype(jnp.bfloat16).reshape(chips, cols, 2 * N)

    home, slot = k // rows, lax.rem(k, rows)

    def row_back(chip):
        return remote(gp.at[chip], grow.at[slot], gp_send.at[chip], gp_recv.at[slot], chip, home)

    def col_back(core):
        lo = pl.ds(0, rows)
        return remote(gp.at[lo], gcol, gp_send.at[chips], gp_recv.at[rows], k, core)

    @pl.when(c == 0)
    def _():
        for d in range(1, chips):
            row_back(lax.rem(k + d, chips)).start()

        @pl.when(home == 1)
        def _():
            row_back(k).start()

        for i in range(rows):

            @pl.when(k == i)
            def _():
                grow[i] = gp[i]

    @pl.when(c == 1)
    def _():
        col_back(0).start()
        gcol[...] = gp[pl.ds(rows, rows)]

    for q in range(depth):
        wgo[q] = weight_block(2 * q + xi)

    def along(q, core):
        return remote(
            zs.at[q, core], zr.at[zi, c], z_send.at[2 * q + core], z_recv.at[2 * zi + c], 2 * q + xi, core
        )

    def forward(q):
        across(q).wait_recv()
        both = wgo[q] + xr[q].astype(jnp.float32)
        wgo[q] = both
        zs[q] = both.astype(jnp.bfloat16).reshape(2, both.shape[0] // 2, both.shape[1])

    def forward_far(q):
        forward(q)
        for core in range(2):
            along(q, core).start()

    def back_project(src, g, w_ref):
        flat = src[...].reshape(rows * cols, 2 * half + 2 * N)
        acc = mm(flat[:, :half], w_ref[g * half : (g + 1) * half, :], NN)
        acc += mm(flat[:, half : 2 * half], w_ref[(2 + g) * half : (3 + g) * half, :], NN)
        at = 4 * half + g * 2 * N
        return acc + mm(flat[:, 2 * half :], w_ref[at : at + 2 * N, :], NN)

    forward_far(order[0])

    @pl.when(c == 0)
    def _():
        col_back(1).wait_recv()

    col_part = [back_project(gcol, 1, w_ref) for w_ref in (wa, wb)]
    for q in order[1:-1]:
        forward_far(q)
    forward(zi)
    along(zi, 1 - c).start()

    for i in range(rows):

        @pl.when(jnp.logical_or(c == 1, k != i))
        def _():
            remote(gp.at[0], grow.at[i], gp_send.at[0], gp_recv.at[i], k, 1 - c).wait_recv()

    for w_ref, at, first in ((wa, mine, col_part[0]), (wb, rest, col_part[1])):
        acc = (first + back_project(grow, 0, w_ref)).reshape(rows, cols, part)
        for i in range(rows):
            flags = flag_ref[i]
            keep = flags[:, 1:2] * (1.0 - flags[:, 0:1])
            pg_ref[i, :, pl.ds(at, part)] = (acc[i] * keep).astype(pg_ref.dtype)

    for q in order[:-1]:
        for core in range(2):
            remote(zs.at[0, 0], zr.at[q, core], z_send.at[0], z_recv.at[2 * q + core], k, 1 - c).wait_recv()
    remote(zs.at[0, 0], zr.at[zi, 1 - c], z_send.at[0], z_recv.at[2 * zi + 1 - c], k, 1 - c).wait_recv()
    zr[zi, c] = zs[zi, c]
    for core in range(2):
        acc = zr[0, core].astype(jnp.float32)
        for q in range(1, depth):
            acc += zr[q, core].astype(jnp.float32)
        out_ref[:, core * half : (core + 1) * half] = acc * scale

    for stream in streams:
        drain(stream)
    weights.wait_send()
    for q in order:
        across(q).wait_send()
    for q in order[:-1]:
        for core in range(2):
            along(q, core).wait_send()
    along(zi, 1 - c).wait_send()

    @pl.when(c == 0)
    def _():
        for d in range(1, chips):
            row_back(lax.rem(k + d, chips)).wait_send()

        @pl.when(home == 1)
        def _():
            row_back(k).wait_send()

    @pl.when(c == 1)
    def _():
        col_back(0).wait_send()


def owned(
    patches, mask_token, masked, tissue, in_weight, out_weight, row_decay, col_decay, cotangent
):
    rows, cols, feat = patches.shape
    chips = lax.axis_size("gcol")
    toks, heads = chips * cols, row_decay.shape[0]
    half, part = out_weight.shape[1], in_weight.shape[1]
    width = 2 * half + 2 * N
    slab = feat // (2 * chips)
    depth = chips // 2
    flags = jnp.stack([masked, tissue], axis=2).astype(jnp.float32)
    bf, fl = jnp.bfloat16, jnp.float32
    vmem, dma = pltpu.VMEM, pltpu.SemaphoreType.DMA
    in_vmem, anywhere = pl.BlockSpec(memory_space=pltpu.VMEM), pl.BlockSpec(memory_space=pl.ANY)
    scale = 1.0 / math.sqrt(2 * rows * cols * chips)
    return pl.pallas_call(
        functools.partial(layer_kernel, chips, rows, scale),
        name="layer",
        out_shape=(
            jax.ShapeDtypeStruct(patches.shape, bf),
            jax.ShapeDtypeStruct((slab, 2 * half), fl),
        ),
        in_specs=[in_vmem] * 6 + [anywhere] * 2,
        out_specs=(in_vmem, in_vmem),
        scratch_shapes=[
            vmem((rows, cols, feat), bf), vmem((rows, cols, feat), bf),
            vmem((rows, heads, cols), fl), vmem((rows, heads, cols), fl),
            vmem((chips, cols, feat), bf), vmem((chips, cols, feat), bf), vmem((chips, heads, cols), fl),
            vmem(in_weight.shape, bf), vmem(in_weight.shape, bf), vmem(out_weight.shape, bf),
            vmem((toks, half), bf), vmem((toks, half), bf), vmem((toks, half), bf),
            vmem((toks, 2 * N), bf), vmem((toks, half), bf), vmem((toks, half), fl),
            vmem((heads, toks, toks), bf), vmem((heads, toks, toks), fl),
            vmem((chips, cols, width), bf), vmem((rows, cols, width), bf), vmem((rows, cols, width), bf),
            vmem((depth, 2 * slab, half), bf), vmem((depth, 2 * slab, half), fl),
            vmem((depth, 2 * slab, half), bf), vmem((depth, 2, slab, half), bf),
            vmem((depth, 2, slab, half), bf),
            dma((rows + 1,)), dma((chips + 1,)), dma((rows + 1,)), dma((chips + 1,)),
            dma((rows + 1,)), dma((chips + 1,)), dma((2,)), dma((2,)),
            dma((chips + 1,)), dma((rows + 1,)), dma((depth,)), dma((depth,)),
            dma((2 * depth,)), dma((2 * depth,)),
        ],
        compiler_params=pltpu.CompilerParams(
            collective_id=0, has_side_effects=True, vmem_limit_bytes=48 << 20
        ),
    )(
        patches, mask_token.reshape(1, feat), cotangent, flags, row_decay, col_decay,
        in_weight, out_weight,
    )


def body(*args):
    rows = args[0].shape[0]
    if lax.axis_size("grow") == 2 and lax.axis_size("gcol") == 2 * rows:
        return owned(*args)
    return shards(*args)


def solution(mesh):
    return jax.shard_map(
        body,
        mesh=mesh,
        in_specs=(
            P(("groups", "grow"), "gcol", None),
            P(),
            P(("groups", "grow"), "gcol"),
            P(("groups", "grow"), "gcol"),
            P(None, "grow"),
            P(None, "grow"),
            P(None, ("groups", "grow"), "gcol"),
            P(None, ("groups", "grow"), "gcol"),
            P(("groups", "grow"), "gcol", None),
        ),
        out_specs=(P(("groups", "grow"), "gcol", None), P(("groups", "gcol", "grow"), None)),
        check_vma=False,
    )
```

```python
import functools
import math

import jax
import jax.numpy as jnp
from jax import lax
from jax.experimental import pallas as pl
from jax.experimental.pallas import tpu as pltpu
from jax.sharding import PartitionSpec as P

E = 1024
HEADS = 16
N = 64


EPSILON = 1e-05
PRECISE = lax.Precision.HIGHEST


def prefix(value, axis, join, neutral):
    count, mine = (lax.axis_size(axis), lax.axis_index(axis))
    pieces = jax.tree.map(lambda part: lax.all_gather(part, axis), value)
    so_far = jax.tree.map(
        lambda part, zero: jnp.full_like(part, 0) + jnp.asarray(zero, part.dtype), value, neutral
    )

    def prefix_hop(position, so_far):
        longer = join(so_far, jax.tree.map(lambda part: part[position], pieces))
        return jax.tree.map(lambda new, old: jnp.where(position < mine, new, old), longer, so_far)

    return lax.fori_loop(0, count - 1, prefix_hop, so_far)


def carried_in(shard, axis, combine, identity):
    length, position = (lax.axis_size(axis), lax.axis_index(axis))
    everything = jax.tree.map(
        lambda part, kind: lax.all_gather(part.astype(kind), axis),
        shard,
        jax.tree.map(lambda a: jnp.bfloat16 if a.dtype == jnp.float32 else a.dtype, shard),
    )
    start = jax.tree.map(
        lambda part, zero: jnp.broadcast_to(jnp.asarray(zero, part.dtype), part.shape),
        shard,
        identity,
    )

    def carried_hop(k, before):
        at = length - 1 - k
        reached = at > position
        new = combine(
            before, jax.tree.map(lambda part, own: part[at].astype(own.dtype), everything, shard)
        )
        return jax.tree.map(lambda a, b: jnp.where(reached, a, b), new, before)

    return lax.fori_loop(0, length, carried_hop, start)


def shortened(shard):

    def short(part):
        return part.astype(jnp.bfloat16) if part.dtype == jnp.float32 else part

    return jax.tree.map(short, shard)


def silu_grad(pre_act):
    sigmoid_v = jax.nn.sigmoid(pre_act)
    return sigmoid_v * (1.0 + pre_act * (1.0 - sigmoid_v))


def per_channel(head_part, channels):
    return jnp.repeat(head_part, channels // head_part.shape[-1], axis=-1)


def line_form(head_lines, channels):
    return per_channel(head_lines.transpose(1, 2, 0), channels)


def carry_on(log_lines, state):
    return per_channel(jnp.exp(log_lines), state.shape[2])[:, None, :] * state


def prepare(log_decay):
    length = log_decay.shape[2]
    running = jnp.cumsum(log_decay, axis=2)
    whole_log = running[:, :, -1]
    causal = jnp.arange(length)[:, None] >= jnp.arange(length)[None, :]
    log_gaps = running[:, :, :, None] - running[:, :, None, :]
    decay_mat = jnp.where(causal, jnp.exp(jnp.where(causal, log_gaps, 0.0)), 0.0)
    return (running, whole_log, decay_mat)


def chain_link(earlier, later):
    return (earlier[0] + later[0], carry_on(later[0], earlier[1]) + later[1])


def split_heads(lines, head_count):
    line_count, length, channels = lines.shape
    return lines.reshape(line_count, length, head_count, channels // head_count)


def local_summary(inputs, key_vecs, prepared):
    running, whole_log, decay_mat = prepared
    to_end = line_form(jnp.exp(whole_log[:, :, None] - running), inputs.shape[2])
    fresh = jnp.einsum("ltc,ltn->lnc", inputs * to_end, key_vecs, precision=PRECISE)
    return (whole_log.T, fresh)


def local_return(query_vecs, prepared, upstream):
    running, whole_log, decay_mat = prepared
    from_start = line_form(jnp.exp(running), upstream.shape[2])
    backward = jnp.einsum("ltc,ltn->lnc", upstream * from_start, query_vecs, precision=PRECISE)
    return (whole_log.T, backward)


def local_outputs(inputs, key_vecs, query_vecs, prepared, incoming):
    running, whole_log, decay_mat = prepared
    head_count = decay_mat.shape[0]
    line_count, length, channels = inputs.shape
    scores = jnp.einsum("ltn,lkn->ltk", query_vecs, key_vecs, precision=PRECISE)
    within = jnp.einsum(
        "gltk,lkgp->ltgp",
        decay_mat * scores[None],
        split_heads(inputs, head_count),
        precision=PRECISE,
    )
    within = within.reshape(line_count, length, channels)
    carried = jnp.einsum("ltn,lnc->ltc", query_vecs, incoming, precision=PRECISE)
    return within + carried * line_form(jnp.exp(running), channels)


def local_grads(inputs, key_vecs, query_vecs, prepared, incoming, returning, upstream):
    running, whole_log, decay_mat = prepared
    head_count = decay_mat.shape[0]
    line_count, length, channels = inputs.shape
    from_start = line_form(jnp.exp(running), channels)
    to_end = line_form(jnp.exp(whole_log[:, :, None] - running), channels)
    scores = jnp.einsum("ltn,lkn->ltk", query_vecs, key_vecs, precision=PRECISE)
    heads_up = split_heads(upstream, head_count)
    heads_in = split_heads(inputs, head_count)
    grad_inputs = jnp.einsum(
        "gltk,ltgp->lkgp", decay_mat * scores[None], heads_up, precision=PRECISE
    ).reshape(line_count, length, channels)
    grad_inputs = (
        grad_inputs + jnp.einsum("lnc,lkn->lkc", returning, key_vecs, precision=PRECISE) * to_end
    )
    mixed = jnp.einsum("ltgp,lkgp->gltk", heads_up, heads_in, precision=PRECISE) * decay_mat
    grad_keys = jnp.einsum("gltk,ltn->lkn", mixed, query_vecs, precision=PRECISE)
    grad_keys = grad_keys + jnp.einsum(
        "lkc,lnc->lkn", inputs * to_end, returning, precision=PRECISE
    )
    grad_queries = jnp.einsum("gltk,lkn->ltn", mixed, key_vecs, precision=PRECISE)
    grad_queries = grad_queries + jnp.einsum(
        "ltc,lnc->ltn", upstream * from_start, incoming, precision=PRECISE
    )
    return (grad_inputs, grad_keys, grad_queries)


def shards(
    patches, mask_token, masked, tissue, in_weight, out_weight, row_decay, col_decay, cotangent
):
    grid_rows, grid_cols, feat_width = patches.shape
    tok_count = grid_rows * grid_cols
    chosen = (masked == 1)[:, :, None]
    present = tissue.astype(jnp.bfloat16)[:, :, None]
    model_in = jnp.where(chosen, mask_token[None, None, :], patches) * present
    flat_in = model_in.reshape(tok_count, feat_width)
    inner_width = E
    half_width = inner_width // 2
    state_size = N
    number_of_heads = HEADS // 2
    offset = 2 * inner_width
    full_in, full_out = (
        lax.all_gather(in_weight, "grow", axis=1, tiled=True),
        lax.all_gather(out_weight, "grow", axis=1, tiled=True),
    )
    projected = lax.dot_general(
        flat_in, full_in, (((1,), (1,)), ((), ())), preferred_element_type=jnp.float32
    )
    proj_bf = projected.astype(jnp.bfloat16)
    pre_values = proj_bf[:, :inner_width].astype(jnp.float32)
    gate_pre = proj_bf[:, inner_width:offset].astype(jnp.float32)
    key_rows = (
        proj_bf[:, offset : offset + state_size]
        .astype(jnp.float32)
        .reshape(grid_rows, grid_cols, state_size)
    )
    query_rows = (
        proj_bf[:, offset + state_size : offset + 2 * state_size]
        .astype(jnp.float32)
        .reshape(grid_rows, grid_cols, state_size)
    )
    key_cols = (
        proj_bf[:, offset + 2 * state_size : offset + 3 * state_size]
        .astype(jnp.float32)
        .reshape(grid_rows, grid_cols, state_size)
        .transpose(1, 0, 2)
    )
    query_cols = (
        proj_bf[:, offset + 3 * state_size : offset + 4 * state_size]
        .astype(jnp.float32)
        .reshape(grid_rows, grid_cols, state_size)
        .transpose(1, 0, 2)
    )
    values = jax.nn.silu(pre_values)
    row_inputs = values[:, :half_width].reshape(grid_rows, grid_cols, half_width)
    col_inputs = values[:, half_width:].reshape(grid_rows, grid_cols, half_width).transpose(1, 0, 2)
    row_prep = prepare(row_decay)
    col_prep = prepare(col_decay.transpose(0, 2, 1))
    row_zero = (
        jnp.zeros((grid_rows, number_of_heads), jnp.float32),
        jnp.zeros((grid_rows, state_size, half_width), jnp.float32),
    )
    col_zero = (
        jnp.zeros((grid_cols, number_of_heads), jnp.float32),
        jnp.zeros((grid_cols, state_size, half_width), jnp.float32),
    )
    row_entry = prefix(local_summary(row_inputs, key_rows, row_prep), "gcol", chain_link, row_zero)[
        1
    ]
    grow_size = lax.axis_size("grow")
    my_block = lax.axis_index("grow")
    parts_in, parts_key, parts_log = (
        lax.all_gather(
            proj_bf[:, half_width:inner_width].reshape(grid_rows, grid_cols, half_width),
            "grow",
            axis=0,
            tiled=True,
        ),
        lax.all_gather(
            proj_bf[:, offset + 2 * state_size : offset + 3 * state_size].reshape(
                grid_rows, grid_cols, state_size
            ),
            "grow",
            axis=0,
            tiled=True,
        ),
        lax.all_gather(
            col_decay.transpose(1, 0, 2).astype(jnp.bfloat16), "grow", axis=0, tiled=True
        ).astype(jnp.float32),
    )
    col_entry = col_zero[1]
    for block_idx in range(grow_size):
        lower_row = block_idx * grid_rows
        piece_in = jax.nn.silu(
            parts_in[lower_row : lower_row + grid_rows].astype(jnp.float32)
        ).transpose(1, 0, 2)
        piece_keys = (
            parts_key[lower_row : lower_row + grid_rows].astype(jnp.float32).transpose(1, 0, 2)
        )
        piece_log = parts_log[lower_row : lower_row + grid_rows].transpose(1, 2, 0)
        whole_log, piece_state = local_summary(piece_in, piece_keys, prepare(piece_log))
        moved = carry_on(whole_log, col_entry) + piece_state
        col_entry = jnp.where(block_idx < my_block, moved, col_entry)
    row_out = local_outputs(row_inputs, key_rows, query_rows, row_prep, row_entry)
    col_out = local_outputs(col_inputs, key_cols, query_cols, col_prep, col_entry).transpose(
        1, 0, 2
    )
    mixed = jnp.concatenate(
        [row_out.reshape(tok_count, half_width), col_out.reshape(tok_count, half_width)], axis=1
    )
    gate_act = jax.nn.silu(gate_pre)
    head_size = inner_width // HEADS
    gated = (mixed * gate_act).reshape(tok_count, HEADS, head_size)
    inv_rms = lax.rsqrt(jnp.mean(gated * gated, axis=2, keepdims=True) + EPSILON)
    normed = gated * inv_rms
    normed_bf = normed.reshape(tok_count, inner_width).astype(jnp.bfloat16)
    grad_out = (cotangent * masked.astype(jnp.bfloat16)[:, :, None]).reshape(tok_count, feat_width)
    total_patches = tok_count * lax.axis_size("gcol") * lax.axis_size("grow")
    weight_sum = lax.psum_scatter(
        lax.dot_general(
            grad_out, normed_bf, (((0,), (0,)), ((), ())), preferred_element_type=jnp.float32
        ),
        ("gcol", "grow"),
        scatter_dimension=0,
        tiled=True,
    )
    out_weight_grad = weight_sum * (1.0 / math.sqrt(total_patches))
    grad_normed_bf = jnp.dot(grad_out, full_out, preferred_element_type=jnp.float32).astype(
        jnp.bfloat16
    )
    grad_normed = lax.optimization_barrier(grad_normed_bf).astype(jnp.float32)
    grad_normed = grad_normed.reshape(tok_count, HEADS, head_size)
    grad_gated = inv_rms * (
        grad_normed - normed * jnp.mean(grad_normed * normed, axis=2, keepdims=True)
    )
    grad_gated = grad_gated.reshape(tok_count, inner_width)
    grad_mixed = grad_gated * gate_act
    grad_gate = grad_gated * mixed * silu_grad(gate_pre)
    row_up = grad_mixed[:, :half_width].reshape(grid_rows, grid_cols, half_width)
    col_up = grad_mixed[:, half_width:].reshape(grid_rows, grid_cols, half_width).transpose(1, 0, 2)
    row_exit = carried_in(local_return(query_rows, row_prep, row_up), "gcol", chain_link, row_zero)[
        1
    ]
    parts_up, parts_query = (
        lax.all_gather(
            shortened(grad_mixed[:, half_width:].reshape(grid_rows, grid_cols, half_width)),
            "grow",
            axis=0,
            tiled=True,
        ),
        lax.all_gather(
            proj_bf[:, offset + 3 * state_size : offset + 4 * state_size].reshape(
                grid_rows, grid_cols, state_size
            ),
            "grow",
            axis=0,
            tiled=True,
        ),
    )
    col_exit = col_zero[1]
    for block_idx in reversed(range(grow_size)):
        lower_row = block_idx * grid_rows
        piece_up = parts_up[lower_row : lower_row + grid_rows].transpose(1, 0, 2)
        piece_queries = (
            parts_query[lower_row : lower_row + grid_rows].astype(jnp.float32).transpose(1, 0, 2)
        )
        piece_log = parts_log[lower_row : lower_row + grid_rows].transpose(1, 2, 0)
        whole_log, piece_back = local_return(piece_queries, prepare(piece_log), piece_up)
        moved = carry_on(whole_log, col_exit) + piece_back
        col_exit = jnp.where(block_idx > my_block, moved, col_exit)
    grad_row_in, grad_row_key, grad_row_query = local_grads(
        row_inputs, key_rows, query_rows, row_prep, row_entry, row_exit, row_up
    )
    grad_col_in, grad_col_key, grad_col_query = local_grads(
        col_inputs, key_cols, query_cols, col_prep, col_entry, col_exit, col_up
    )
    grad_values = jnp.concatenate(
        [
            grad_row_in.reshape(tok_count, half_width),
            grad_col_in.transpose(1, 0, 2).reshape(tok_count, half_width),
        ],
        axis=1,
    )
    grad_proj = jnp.concatenate(
        [
            grad_values * silu_grad(pre_values),
            grad_gate,
            grad_row_key.reshape(tok_count, state_size),
            grad_row_query.reshape(tok_count, state_size),
            grad_col_key.transpose(1, 0, 2).reshape(tok_count, state_size),
            grad_col_query.transpose(1, 0, 2).reshape(tok_count, state_size),
        ],
        axis=1,
    ).astype(jnp.bfloat16)
    keep_mask = present * (1 - masked).astype(jnp.bfloat16)[:, :, None]
    grad_model_in = jnp.dot(grad_proj, full_in, preferred_element_type=jnp.float32).reshape(
        grid_rows, grid_cols, feat_width
    )
    patch_grad = (grad_model_in * keep_mask).astype(jnp.bfloat16)
    return (patch_grad, out_weight_grad)


MESH = pl.DeviceIdType.MESH
NT = (((1,), (1,)), ((), ()))
NN = (((1,), (0,)), ((), ()))
TN = (((0,), (0,)), ((), ()))


def mm(a, b, dims):
    return lax.dot_general(a, b, dims, preferred_element_type=jnp.float32)


def layer_kernel(
    chips, rows, scale,
    patch_hbm, token_hbm, cot_hbm, hidden_hbm, present_hbm, rdec_hbm, cdec_hbm, w_hbm, wout_hbm,
    pg_ref, out_ref,
    patch_ref, token_ref, cot_ref, hidden_ref, present_ref, rdec_ref, cdec_ref, in_sem,
    xs, gs, rd, cd, xb, gb, db, wa, wb, wout, u_s, z_s, gn_s, bc_s, normed_s, y_s, mat_s, dec_s, gp, grow, gcol,
    xsend, wgo, xr, zs, zr,
    x_send, x_recv, g_send, g_recv, d_send, d_recv, w_sem, l_sem,
    gp_send, gp_recv, xr_send, xr_recv, z_send, z_recv,
):
    k, c = lax.axis_index("gcol"), lax.axis_index("grow")
    depth = chips // 2
    zi, xi = k // 2, lax.rem(k, 2)
    cols, feat = xs.shape[1], xs.shape[2]
    toks = chips * cols
    half, part = wout.shape[1], wa.shape[1]
    total = 2 * chips

    load_w = pltpu.make_async_copy(w_hbm, wa, l_sem.at[0])
    load_o = pltpu.make_async_copy(wout_hbm, wout, l_sem.at[1])
    loads = [
        pltpu.make_async_copy(src, dst, in_sem.at[i])
        for i, (src, dst) in enumerate(
            (
                (hidden_hbm, hidden_ref), (present_hbm, present_ref), (token_hbm, token_ref),
                (patch_hbm, patch_ref), (rdec_hbm, rdec_ref), (cdec_hbm, cdec_ref), (cot_hbm, cot_ref),
            )
        )
    ]
    for copy in loads:
        copy.start()
    load_w.start()
    load_o.start()

    me = 2 * k + c
    barrier = pltpu.get_barrier_semaphore()
    for d in range(1, total):
        to = lax.rem(me + d, total)
        pl.semaphore_signal(
            barrier, inc=1, device_id={"gcol": to // 2, "grow": lax.rem(to, 2)}, device_id_type=MESH
        )

    def remote(src, dst, s, r, chip, core):
        return pltpu.make_async_remote_copy(
            src_ref=src, dst_ref=dst, send_sem=s, recv_sem=r,
            device_id={"gcol": chip, "grow": core}, device_id_type=MESH,
        )

    for copy in loads[:-1]:
        copy.wait()
    square = (cols, cols)
    eye = lax.broadcasted_iota(jnp.int32, square, 0) == lax.broadcasted_iota(jnp.int32, square, 1)
    eye = eye.astype(jnp.float32)
    hidden_t = mm(eye, hidden_ref[...].astype(jnp.float32), NT)
    present_t = mm(eye, present_ref[...].astype(jnp.float32), NT)
    token = token_ref[...].reshape(1, feat).astype(jnp.float32)
    for i in range(rows):
        hidden, present = hidden_t[:, i : i + 1], present_t[:, i : i + 1]
        chosen = jnp.where(hidden > 0.5, token, patch_ref[i].astype(jnp.float32))
        xs[i] = (chosen * present).astype(jnp.bfloat16)
        rd[i] = rdec_ref[:, i, :]
        cd[i] = cdec_ref[:, i, :]

    streams = (
        (xs, xs, xb, x_send, x_recv),
        (rd, cd, db, d_send, d_recv),
        (gs, gs, gb, g_send, g_recv),
    )

    def row_out(stream, i):
        row_src, _, dst, s, r = stream
        return remote(row_src.at[i], dst.at[k], s.at[i], r.at[k], rows * c + i, 0)

    def col_out(stream):
        _, col_src, dst, s, r = stream
        return remote(col_src, dst.at[pl.ds(0, rows)], s.at[rows], r.at[chips], k, 1)

    def row_in(stream, src):
        row_src, _, dst, s, r = stream
        return remote(row_src.at[0], dst.at[src], s.at[0], r.at[src], k, 1 - c)

    def col_in(stream):
        _, col_src, dst, s, r = stream
        return remote(col_src, dst.at[pl.ds(0, rows)], s.at[rows], r.at[chips], k, 1 - c)

    def launch(stream):
        for i in range(rows):

            @pl.when(jnp.logical_or(c == 1, k != i))
            def _():
                row_out(stream, i).start()

        @pl.when(c == 0)
        def _():
            col_out(stream).start()

    def arrive(stream):
        @pl.when(c == 0)
        def _():
            for d in range(1, chips):
                row_in(stream, lax.rem(k + d, chips)).wait_recv()

            @pl.when(k >= rows)
            def _():
                row_in(stream, k).wait_recv()

        @pl.when(c == 1)
        def _():
            col_in(stream).wait_recv()

    def drain(stream):
        for i in range(rows):

            @pl.when(jnp.logical_or(c == 1, k != i))
            def _():
                row_out(stream, i).wait_send()

        @pl.when(c == 0)
        def _():
            col_out(stream).wait_send()

    pl.semaphore_wait(barrier, total - 1)
    weights = remote(w_hbm, wb, w_sem.at[0], w_sem.at[1], k, 1 - c)
    launch(streams[0])
    launch(streams[1])
    weights.start()
    loads[-1].wait()
    for i in range(rows):
        gs[i] = (cot_ref[i].astype(jnp.float32) * hidden_t[:, i : i + 1]).astype(jnp.bfloat16)
    launch(streams[2])

    for row_src, col_src, dst, _, _ in streams:

        @pl.when(c == 1)
        def _():
            dst[pl.ds(rows, rows)] = col_src[...]

        for i in range(rows):

            @pl.when(jnp.logical_and(c == 0, k == i))
            def _():
                dst[i] = row_src[i]

    t_at = lax.broadcasted_iota(jnp.int32, (toks, toks), 0)
    k_at = lax.broadcasted_iota(jnp.int32, (toks, toks), 1)
    step = jnp.where(c == 0, 1, cols)
    mask = jnp.logical_and(t_at >= k_at, lax.rem(t_at, step) == lax.rem(k_at, step))
    low = lax.broadcasted_iota(jnp.int32, (toks, 128), 1) < N

    arrive(streams[1])
    ones = mask.astype(jnp.float32)
    dec = jnp.concatenate([db[i] for i in range(chips)], axis=1)
    run_s = lax.dot_general(ones, dec, NT, precision=PRECISE, preferred_element_type=jnp.float32)
    run_l = lax.dot_general(dec, ones, NT, precision=PRECISE, preferred_element_type=jnp.float32)
    heads = dec.shape[0]
    for h in range(heads):
        gap = run_s[:, h : h + 1] - run_l[h : h + 1, :]
        dec_s[h] = jnp.where(mask, jnp.exp(jnp.minimum(gap, 0.0)), 0.0)

    load_w.wait()
    arrive(streams[0])
    mine, rest = pl.multiple_of(c * part, part), pl.multiple_of((1 - c) * part, part)
    own = xb[:, :, pl.ds(mine, part)].reshape(toks, part)
    oth = xb[:, :, pl.ds(rest, part)].reshape(toks, part)
    pieces = ((u_s, c * half, half), (z_s, 2 * half + c * half, half), (bc_s, 4 * half + c * 2 * N, 2 * N))
    partial = [
        mm(own, wa[pl.ds(pl.multiple_of(start, 128), size), :], NT) for _, start, size in pieces
    ]
    weights.wait_recv()
    for (dst, start, size), first in zip(pieces, partial):
        second = mm(oth, wb[pl.ds(pl.multiple_of(start, 128), size), :], NT)
        dst[...] = (first + second).astype(jnp.bfloat16)

    b_bf, c_bf = bc_s[:, :N], bc_s[:, N:]
    scores = mm(c_bf, b_bf, NT)

    def per_head(x):
        first = jnp.sum(jnp.where(low, x, 0.0), axis=1, keepdims=True)
        second = jnp.sum(jnp.where(low, 0.0, x), axis=1, keepdims=True)
        return jnp.where(low, first, second) * (1.0 / N)

    def norm(p):
        cols_p = slice(p * 128, (p + 1) * 128)
        z = z_s[:, cols_p].astype(jnp.float32)
        sig_z = 1.0 / (1.0 + jnp.exp(-z))
        y = y_s[:, cols_p]
        gated = y * (z * sig_z)
        inv = lax.rsqrt(per_head(gated * gated) + EPSILON)
        return cols_p, z, sig_z, y, inv, gated * inv

    for p in range(half // 128):
        cols_p = slice(p * 128, (p + 1) * 128)
        u = u_s[:, cols_p].astype(jnp.float32)
        val_bf = (u / (1.0 + jnp.exp(-u))).astype(jnp.bfloat16)
        for h in (2 * p, 2 * p + 1):
            mat_s[h] = (dec_s[h] * scores).astype(jnp.bfloat16)
        y_s[:, cols_p] = jnp.where(
            low, mm(mat_s[2 * p], val_bf, NN), mm(mat_s[2 * p + 1], val_bf, NN)
        )
        normed_s[:, cols_p] = norm(p)[-1].astype(jnp.bfloat16)

    load_o.wait()
    arrive(streams[2])

    def weight_block(chip):
        at = pl.ds(pl.multiple_of(chip * 128, 128), 128)
        return mm(gb[:, :, at].reshape(toks, 128), normed_s[...], TN)

    def across(q):
        return remote(xsend.at[q], xr.at[q], xr_send.at[q], xr_recv.at[q], 2 * zi + 1 - xi, c)

    order = [lax.rem(zi + 1 + j, depth) for j in range(depth)]
    for q in order:
        xsend[q] = weight_block(2 * q + 1 - xi).astype(jnp.bfloat16)
        across(q).start()

    grads = gb[...].reshape(toks, feat)
    gn_s[...] = mm(grads, wout[...], NN).astype(jnp.bfloat16)
    d_scores = jnp.zeros((toks, toks), jnp.float32)
    for p in range(half // 128):
        cols_p, z, sig_z, y, inv, normed = norm(p)
        u = u_s[:, cols_p].astype(jnp.float32)
        sig_u = 1.0 / (1.0 + jnp.exp(-u))
        val_bf = (u * sig_u).astype(jnp.bfloat16)
        gn = gn_s[:, cols_p].astype(jnp.float32)
        gg = inv * (gn - normed * per_head(gn * normed))
        dy = gg * (z * sig_z)
        dz = gg * y * (sig_z * (1.0 + z * (1.0 - sig_z)))
        dy_bf = dy.astype(jnp.bfloat16)
        dv = jnp.where(low, mm(mat_s[2 * p], dy_bf, TN), mm(mat_s[2 * p + 1], dy_bf, TN))
        du = dv * (sig_u * (1.0 + u * (1.0 - sig_u)))
        gp[:, :, cols_p] = du.astype(jnp.bfloat16).reshape(chips, cols, 128)
        gp[:, :, half + p * 128 : half + (p + 1) * 128] = dz.astype(jnp.bfloat16).reshape(
            chips, cols, 128
        )
        zero = jnp.zeros_like(dy)
        d_scores += dec_s[2 * p] * mm(jnp.where(low, dy, zero).astype(jnp.bfloat16), val_bf, NT)
        d_scores += dec_s[2 * p + 1] * mm(jnp.where(low, zero, dy).astype(jnp.bfloat16), val_bf, NT)
    ds_bf = d_scores.astype(jnp.bfloat16)
    d_bc = jnp.concatenate([mm(ds_bf, c_bf, TN), mm(ds_bf, b_bf, NN)], axis=1)
    gp[:, :, 2 * half :] = d_bc.astype(jnp.bfloat16).reshape(chips, cols, 2 * N)

    home, slot = k // rows, lax.rem(k, rows)

    def row_back(chip):
        return remote(gp.at[chip], grow.at[slot], gp_send.at[chip], gp_recv.at[slot], chip, home)

    def col_back(core):
        lo = pl.ds(0, rows)
        return remote(gp.at[lo], gcol, gp_send.at[chips], gp_recv.at[rows], k, core)

    @pl.when(c == 0)
    def _():
        for d in range(1, chips):
            row_back(lax.rem(k + d, chips)).start()

        @pl.when(home == 1)
        def _():
            row_back(k).start()

        for i in range(rows):

            @pl.when(k == i)
            def _():
                grow[i] = gp[i]

    @pl.when(c == 1)
    def _():
        col_back(0).start()
        gcol[...] = gp[pl.ds(rows, rows)]

    for q in range(depth):
        wgo[q] = weight_block(2 * q + xi)

    def along(q, core):
        return remote(
            zs.at[q, core], zr.at[zi, c], z_send.at[2 * q + core], z_recv.at[2 * zi + c], 2 * q + xi, core
        )

    def forward(q):
        across(q).wait_recv()
        both = wgo[q] + xr[q].astype(jnp.float32)
        wgo[q] = both
        zs[q] = both.astype(jnp.bfloat16).reshape(2, both.shape[0] // 2, both.shape[1])

    def forward_far(q):
        forward(q)
        for core in range(2):
            along(q, core).start()

    def back_project(src, g, w_ref):
        flat = src[...].reshape(rows * cols, 2 * half + 2 * N)
        acc = mm(flat[:, :half], w_ref[g * half : (g + 1) * half, :], NN)
        acc += mm(flat[:, half : 2 * half], w_ref[(2 + g) * half : (3 + g) * half, :], NN)
        at = 4 * half + g * 2 * N
        return acc + mm(flat[:, 2 * half :], w_ref[at : at + 2 * N, :], NN)

    forward_far(order[0])

    @pl.when(c == 0)
    def _():
        col_back(1).wait_recv()

    col_part = [back_project(gcol, 1, w_ref) for w_ref in (wa, wb)]
    for q in order[1:-1]:
        forward_far(q)
    forward(zi)
    along(zi, 1 - c).start()

    for i in range(rows):

        @pl.when(jnp.logical_or(c == 1, k != i))
        def _():
            remote(gp.at[0], grow.at[i], gp_send.at[0], gp_recv.at[i], k, 1 - c).wait_recv()

    for w_ref, at, first in ((wa, mine, col_part[0]), (wb, rest, col_part[1])):
        acc = (first + back_project(grow, 0, w_ref)).reshape(rows, cols, part)
        for i in range(rows):
            keep = present_t[:, i : i + 1] * (1.0 - hidden_t[:, i : i + 1])
            pg_ref[i, :, pl.ds(at, part)] = (acc[i] * keep).astype(pg_ref.dtype)

    for q in order[:-1]:
        for core in range(2):
            remote(zs.at[0, 0], zr.at[q, core], z_send.at[0], z_recv.at[2 * q + core], k, 1 - c).wait_recv()
    remote(zs.at[0, 0], zr.at[zi, 1 - c], z_send.at[0], z_recv.at[2 * zi + 1 - c], k, 1 - c).wait_recv()
    zr[zi, c] = zs[zi, c]
    for core in range(2):
        acc = zr[0, core].astype(jnp.float32)
        for q in range(1, depth):
            acc += zr[q, core].astype(jnp.float32)
        out_ref[:, core * half : (core + 1) * half] = acc * scale

    for stream in streams:
        drain(stream)
    weights.wait_send()
    for q in order:
        across(q).wait_send()
    for q in order[:-1]:
        for core in range(2):
            along(q, core).wait_send()
    along(zi, 1 - c).wait_send()

    @pl.when(c == 0)
    def _():
        for d in range(1, chips):
            row_back(lax.rem(k + d, chips)).wait_send()

        @pl.when(home == 1)
        def _():
            row_back(k).wait_send()

    @pl.when(c == 1)
    def _():
        col_back(0).wait_send()


def owned(
    patches, mask_token, masked, tissue, in_weight, out_weight, row_decay, col_decay, cotangent
):
    rows, cols, feat = patches.shape
    chips = lax.axis_size("gcol")
    toks, heads = chips * cols, row_decay.shape[0]
    half, part = out_weight.shape[1], in_weight.shape[1]
    width = 2 * half + 2 * N
    slab = feat // (2 * chips)
    depth = chips // 2
    bf, fl = jnp.bfloat16, jnp.float32
    vmem, dma = pltpu.VMEM, pltpu.SemaphoreType.DMA
    in_vmem, anywhere = pl.BlockSpec(memory_space=pltpu.VMEM), pl.BlockSpec(memory_space=pltpu.HBM)
    scale = 1.0 / math.sqrt(2 * rows * cols * chips)
    return pl.pallas_call(
        functools.partial(layer_kernel, chips, rows, scale),
        name="layer",
        out_shape=(
            jax.ShapeDtypeStruct(patches.shape, bf),
            jax.ShapeDtypeStruct((slab, 2 * half), fl),
        ),
        in_specs=[anywhere] * 9,
        out_specs=(in_vmem, in_vmem),
        scratch_shapes=[
            vmem(patches.shape, bf), vmem(mask_token.shape, bf), vmem(patches.shape, bf),
            vmem(masked.shape, masked.dtype), vmem(tissue.shape, tissue.dtype),
            vmem(row_decay.shape, fl), vmem(col_decay.shape, fl), dma((7,)),
            vmem((rows, cols, feat), bf), vmem((rows, cols, feat), bf),
            vmem((rows, heads, cols), fl), vmem((rows, heads, cols), fl),
            vmem((chips, cols, feat), bf), vmem((chips, cols, feat), bf), vmem((chips, heads, cols), fl),
            vmem(in_weight.shape, bf), vmem(in_weight.shape, bf), vmem(out_weight.shape, bf),
            vmem((toks, half), bf), vmem((toks, half), bf), vmem((toks, half), bf),
            vmem((toks, 2 * N), bf), vmem((toks, half), bf), vmem((toks, half), fl),
            vmem((heads, toks, toks), bf), vmem((heads, toks, toks), fl),
            vmem((chips, cols, width), bf), vmem((rows, cols, width), bf), vmem((rows, cols, width), bf),
            vmem((depth, 2 * slab, half), bf), vmem((depth, 2 * slab, half), fl),
            vmem((depth, 2 * slab, half), bf), vmem((depth, 2, slab, half), bf),
            vmem((depth, 2, slab, half), bf),
            dma((rows + 1,)), dma((chips + 1,)), dma((rows + 1,)), dma((chips + 1,)),
            dma((rows + 1,)), dma((chips + 1,)), dma((2,)), dma((2,)),
            dma((chips + 1,)), dma((rows + 1,)), dma((depth,)), dma((depth,)),
            dma((2 * depth,)), dma((2 * depth,)),
        ],
        compiler_params=pltpu.CompilerParams(
            collective_id=0, has_side_effects=True, vmem_limit_bytes=60 << 20
        ),
    )(
        patches, mask_token, cotangent, masked, tissue, row_decay, col_decay,
        in_weight, out_weight,
    )


def body(*args):
    rows = args[0].shape[0]
    if lax.axis_size("grow") == 2 and lax.axis_size("gcol") == 2 * rows:
        return owned(*args)
    return shards(*args)


def solution(mesh):
    return jax.shard_map(
        body,
        mesh=mesh,
        in_specs=(
            P(("groups", "grow"), "gcol", None),
            P(),
            P(("groups", "grow"), "gcol"),
            P(("groups", "grow"), "gcol"),
            P(None, "grow"),
            P(None, "grow"),
            P(None, ("groups", "grow"), "gcol"),
            P(None, ("groups", "grow"), "gcol"),
            P(("groups", "grow"), "gcol", None),
        ),
        out_specs=(P(("groups", "grow"), "gcol", None), P(("groups", "gcol", "grow"), None)),
        check_vma=False,
    )
```

```python
import functools
import math

import jax
import jax.numpy as jnp
from jax import lax
from jax.experimental import pallas as pl
from jax.experimental.pallas import tpu as pltpu
from jax.sharding import PartitionSpec as P

E = 1024
HEADS = 16
N = 64


EPSILON = 1e-05
PRECISE = lax.Precision.HIGHEST


def prefix(value, axis, join, neutral):
    count, mine = (lax.axis_size(axis), lax.axis_index(axis))
    pieces = jax.tree.map(lambda part: lax.all_gather(part, axis), value)
    so_far = jax.tree.map(
        lambda part, zero: jnp.full_like(part, 0) + jnp.asarray(zero, part.dtype), value, neutral
    )

    def prefix_hop(position, so_far):
        longer = join(so_far, jax.tree.map(lambda part: part[position], pieces))
        return jax.tree.map(lambda new, old: jnp.where(position < mine, new, old), longer, so_far)

    return lax.fori_loop(0, count - 1, prefix_hop, so_far)


def carried_in(shard, axis, combine, identity):
    length, position = (lax.axis_size(axis), lax.axis_index(axis))
    everything = jax.tree.map(
        lambda part, kind: lax.all_gather(part.astype(kind), axis),
        shard,
        jax.tree.map(lambda a: jnp.bfloat16 if a.dtype == jnp.float32 else a.dtype, shard),
    )
    start = jax.tree.map(
        lambda part, zero: jnp.broadcast_to(jnp.asarray(zero, part.dtype), part.shape),
        shard,
        identity,
    )

    def carried_hop(k, before):
        at = length - 1 - k
        reached = at > position
        new = combine(
            before, jax.tree.map(lambda part, own: part[at].astype(own.dtype), everything, shard)
        )
        return jax.tree.map(lambda a, b: jnp.where(reached, a, b), new, before)

    return lax.fori_loop(0, length, carried_hop, start)


def shortened(shard):

    def short(part):
        return part.astype(jnp.bfloat16) if part.dtype == jnp.float32 else part

    return jax.tree.map(short, shard)


def silu_grad(pre_act):
    sigmoid_v = jax.nn.sigmoid(pre_act)
    return sigmoid_v * (1.0 + pre_act * (1.0 - sigmoid_v))


def per_channel(head_part, channels):
    return jnp.repeat(head_part, channels // head_part.shape[-1], axis=-1)


def line_form(head_lines, channels):
    return per_channel(head_lines.transpose(1, 2, 0), channels)


def carry_on(log_lines, state):
    return per_channel(jnp.exp(log_lines), state.shape[2])[:, None, :] * state


def prepare(log_decay):
    length = log_decay.shape[2]
    running = jnp.cumsum(log_decay, axis=2)
    whole_log = running[:, :, -1]
    causal = jnp.arange(length)[:, None] >= jnp.arange(length)[None, :]
    log_gaps = running[:, :, :, None] - running[:, :, None, :]
    decay_mat = jnp.where(causal, jnp.exp(jnp.where(causal, log_gaps, 0.0)), 0.0)
    return (running, whole_log, decay_mat)


def chain_link(earlier, later):
    return (earlier[0] + later[0], carry_on(later[0], earlier[1]) + later[1])


def split_heads(lines, head_count):
    line_count, length, channels = lines.shape
    return lines.reshape(line_count, length, head_count, channels // head_count)


def local_summary(inputs, key_vecs, prepared):
    running, whole_log, decay_mat = prepared
    to_end = line_form(jnp.exp(whole_log[:, :, None] - running), inputs.shape[2])
    fresh = jnp.einsum("ltc,ltn->lnc", inputs * to_end, key_vecs, precision=PRECISE)
    return (whole_log.T, fresh)


def local_return(query_vecs, prepared, upstream):
    running, whole_log, decay_mat = prepared
    from_start = line_form(jnp.exp(running), upstream.shape[2])
    backward = jnp.einsum("ltc,ltn->lnc", upstream * from_start, query_vecs, precision=PRECISE)
    return (whole_log.T, backward)


def local_outputs(inputs, key_vecs, query_vecs, prepared, incoming):
    running, whole_log, decay_mat = prepared
    head_count = decay_mat.shape[0]
    line_count, length, channels = inputs.shape
    scores = jnp.einsum("ltn,lkn->ltk", query_vecs, key_vecs, precision=PRECISE)
    within = jnp.einsum(
        "gltk,lkgp->ltgp",
        decay_mat * scores[None],
        split_heads(inputs, head_count),
        precision=PRECISE,
    )
    within = within.reshape(line_count, length, channels)
    carried = jnp.einsum("ltn,lnc->ltc", query_vecs, incoming, precision=PRECISE)
    return within + carried * line_form(jnp.exp(running), channels)


def local_grads(inputs, key_vecs, query_vecs, prepared, incoming, returning, upstream):
    running, whole_log, decay_mat = prepared
    head_count = decay_mat.shape[0]
    line_count, length, channels = inputs.shape
    from_start = line_form(jnp.exp(running), channels)
    to_end = line_form(jnp.exp(whole_log[:, :, None] - running), channels)
    scores = jnp.einsum("ltn,lkn->ltk", query_vecs, key_vecs, precision=PRECISE)
    heads_up = split_heads(upstream, head_count)
    heads_in = split_heads(inputs, head_count)
    grad_inputs = jnp.einsum(
        "gltk,ltgp->lkgp", decay_mat * scores[None], heads_up, precision=PRECISE
    ).reshape(line_count, length, channels)
    grad_inputs = (
        grad_inputs + jnp.einsum("lnc,lkn->lkc", returning, key_vecs, precision=PRECISE) * to_end
    )
    mixed = jnp.einsum("ltgp,lkgp->gltk", heads_up, heads_in, precision=PRECISE) * decay_mat
    grad_keys = jnp.einsum("gltk,ltn->lkn", mixed, query_vecs, precision=PRECISE)
    grad_keys = grad_keys + jnp.einsum(
        "lkc,lnc->lkn", inputs * to_end, returning, precision=PRECISE
    )
    grad_queries = jnp.einsum("gltk,lkn->ltn", mixed, key_vecs, precision=PRECISE)
    grad_queries = grad_queries + jnp.einsum(
        "ltc,lnc->ltn", upstream * from_start, incoming, precision=PRECISE
    )
    return (grad_inputs, grad_keys, grad_queries)


def shards(
    patches, mask_token, masked, tissue, in_weight, out_weight, row_decay, col_decay, cotangent
):
    grid_rows, grid_cols, feat_width = patches.shape
    tok_count = grid_rows * grid_cols
    chosen = (masked == 1)[:, :, None]
    present = tissue.astype(jnp.bfloat16)[:, :, None]
    model_in = jnp.where(chosen, mask_token[None, None, :], patches) * present
    flat_in = model_in.reshape(tok_count, feat_width)
    inner_width = E
    half_width = inner_width // 2
    state_size = N
    number_of_heads = HEADS // 2
    offset = 2 * inner_width
    full_in, full_out = (
        lax.all_gather(in_weight, "grow", axis=1, tiled=True),
        lax.all_gather(out_weight, "grow", axis=1, tiled=True),
    )
    projected = lax.dot_general(
        flat_in, full_in, (((1,), (1,)), ((), ())), preferred_element_type=jnp.float32
    )
    proj_bf = projected.astype(jnp.bfloat16)
    pre_values = proj_bf[:, :inner_width].astype(jnp.float32)
    gate_pre = proj_bf[:, inner_width:offset].astype(jnp.float32)
    key_rows = (
        proj_bf[:, offset : offset + state_size]
        .astype(jnp.float32)
        .reshape(grid_rows, grid_cols, state_size)
    )
    query_rows = (
        proj_bf[:, offset + state_size : offset + 2 * state_size]
        .astype(jnp.float32)
        .reshape(grid_rows, grid_cols, state_size)
    )
    key_cols = (
        proj_bf[:, offset + 2 * state_size : offset + 3 * state_size]
        .astype(jnp.float32)
        .reshape(grid_rows, grid_cols, state_size)
        .transpose(1, 0, 2)
    )
    query_cols = (
        proj_bf[:, offset + 3 * state_size : offset + 4 * state_size]
        .astype(jnp.float32)
        .reshape(grid_rows, grid_cols, state_size)
        .transpose(1, 0, 2)
    )
    values = jax.nn.silu(pre_values)
    row_inputs = values[:, :half_width].reshape(grid_rows, grid_cols, half_width)
    col_inputs = values[:, half_width:].reshape(grid_rows, grid_cols, half_width).transpose(1, 0, 2)
    row_prep = prepare(row_decay)
    col_prep = prepare(col_decay.transpose(0, 2, 1))
    row_zero = (
        jnp.zeros((grid_rows, number_of_heads), jnp.float32),
        jnp.zeros((grid_rows, state_size, half_width), jnp.float32),
    )
    col_zero = (
        jnp.zeros((grid_cols, number_of_heads), jnp.float32),
        jnp.zeros((grid_cols, state_size, half_width), jnp.float32),
    )
    row_entry = prefix(local_summary(row_inputs, key_rows, row_prep), "gcol", chain_link, row_zero)[
        1
    ]
    grow_size = lax.axis_size("grow")
    my_block = lax.axis_index("grow")
    parts_in, parts_key, parts_log = (
        lax.all_gather(
            proj_bf[:, half_width:inner_width].reshape(grid_rows, grid_cols, half_width),
            "grow",
            axis=0,
            tiled=True,
        ),
        lax.all_gather(
            proj_bf[:, offset + 2 * state_size : offset + 3 * state_size].reshape(
                grid_rows, grid_cols, state_size
            ),
            "grow",
            axis=0,
            tiled=True,
        ),
        lax.all_gather(
            col_decay.transpose(1, 0, 2).astype(jnp.bfloat16), "grow", axis=0, tiled=True
        ).astype(jnp.float32),
    )
    col_entry = col_zero[1]
    for block_idx in range(grow_size):
        lower_row = block_idx * grid_rows
        piece_in = jax.nn.silu(
            parts_in[lower_row : lower_row + grid_rows].astype(jnp.float32)
        ).transpose(1, 0, 2)
        piece_keys = (
            parts_key[lower_row : lower_row + grid_rows].astype(jnp.float32).transpose(1, 0, 2)
        )
        piece_log = parts_log[lower_row : lower_row + grid_rows].transpose(1, 2, 0)
        whole_log, piece_state = local_summary(piece_in, piece_keys, prepare(piece_log))
        moved = carry_on(whole_log, col_entry) + piece_state
        col_entry = jnp.where(block_idx < my_block, moved, col_entry)
    row_out = local_outputs(row_inputs, key_rows, query_rows, row_prep, row_entry)
    col_out = local_outputs(col_inputs, key_cols, query_cols, col_prep, col_entry).transpose(
        1, 0, 2
    )
    mixed = jnp.concatenate(
        [row_out.reshape(tok_count, half_width), col_out.reshape(tok_count, half_width)], axis=1
    )
    gate_act = jax.nn.silu(gate_pre)
    head_size = inner_width // HEADS
    gated = (mixed * gate_act).reshape(tok_count, HEADS, head_size)
    inv_rms = lax.rsqrt(jnp.mean(gated * gated, axis=2, keepdims=True) + EPSILON)
    normed = gated * inv_rms
    normed_bf = normed.reshape(tok_count, inner_width).astype(jnp.bfloat16)
    grad_out = (cotangent * masked.astype(jnp.bfloat16)[:, :, None]).reshape(tok_count, feat_width)
    total_patches = tok_count * lax.axis_size("gcol") * lax.axis_size("grow")
    weight_sum = lax.psum_scatter(
        lax.dot_general(
            grad_out, normed_bf, (((0,), (0,)), ((), ())), preferred_element_type=jnp.float32
        ),
        ("gcol", "grow"),
        scatter_dimension=0,
        tiled=True,
    )
    out_weight_grad = weight_sum * (1.0 / math.sqrt(total_patches))
    grad_normed_bf = jnp.dot(grad_out, full_out, preferred_element_type=jnp.float32).astype(
        jnp.bfloat16
    )
    grad_normed = lax.optimization_barrier(grad_normed_bf).astype(jnp.float32)
    grad_normed = grad_normed.reshape(tok_count, HEADS, head_size)
    grad_gated = inv_rms * (
        grad_normed - normed * jnp.mean(grad_normed * normed, axis=2, keepdims=True)
    )
    grad_gated = grad_gated.reshape(tok_count, inner_width)
    grad_mixed = grad_gated * gate_act
    grad_gate = grad_gated * mixed * silu_grad(gate_pre)
    row_up = grad_mixed[:, :half_width].reshape(grid_rows, grid_cols, half_width)
    col_up = grad_mixed[:, half_width:].reshape(grid_rows, grid_cols, half_width).transpose(1, 0, 2)
    row_exit = carried_in(local_return(query_rows, row_prep, row_up), "gcol", chain_link, row_zero)[
        1
    ]
    parts_up, parts_query = (
        lax.all_gather(
            shortened(grad_mixed[:, half_width:].reshape(grid_rows, grid_cols, half_width)),
            "grow",
            axis=0,
            tiled=True,
        ),
        lax.all_gather(
            proj_bf[:, offset + 3 * state_size : offset + 4 * state_size].reshape(
                grid_rows, grid_cols, state_size
            ),
            "grow",
            axis=0,
            tiled=True,
        ),
    )
    col_exit = col_zero[1]
    for block_idx in reversed(range(grow_size)):
        lower_row = block_idx * grid_rows
        piece_up = parts_up[lower_row : lower_row + grid_rows].transpose(1, 0, 2)
        piece_queries = (
            parts_query[lower_row : lower_row + grid_rows].astype(jnp.float32).transpose(1, 0, 2)
        )
        piece_log = parts_log[lower_row : lower_row + grid_rows].transpose(1, 2, 0)
        whole_log, piece_back = local_return(piece_queries, prepare(piece_log), piece_up)
        moved = carry_on(whole_log, col_exit) + piece_back
        col_exit = jnp.where(block_idx > my_block, moved, col_exit)
    grad_row_in, grad_row_key, grad_row_query = local_grads(
        row_inputs, key_rows, query_rows, row_prep, row_entry, row_exit, row_up
    )
    grad_col_in, grad_col_key, grad_col_query = local_grads(
        col_inputs, key_cols, query_cols, col_prep, col_entry, col_exit, col_up
    )
    grad_values = jnp.concatenate(
        [
            grad_row_in.reshape(tok_count, half_width),
            grad_col_in.transpose(1, 0, 2).reshape(tok_count, half_width),
        ],
        axis=1,
    )
    grad_proj = jnp.concatenate(
        [
            grad_values * silu_grad(pre_values),
            grad_gate,
            grad_row_key.reshape(tok_count, state_size),
            grad_row_query.reshape(tok_count, state_size),
            grad_col_key.transpose(1, 0, 2).reshape(tok_count, state_size),
            grad_col_query.transpose(1, 0, 2).reshape(tok_count, state_size),
        ],
        axis=1,
    ).astype(jnp.bfloat16)
    keep_mask = present * (1 - masked).astype(jnp.bfloat16)[:, :, None]
    grad_model_in = jnp.dot(grad_proj, full_in, preferred_element_type=jnp.float32).reshape(
        grid_rows, grid_cols, feat_width
    )
    patch_grad = (grad_model_in * keep_mask).astype(jnp.bfloat16)
    return (patch_grad, out_weight_grad)


MESH = pl.DeviceIdType.MESH
NT = (((1,), (1,)), ((), ()))
NN = (((1,), (0,)), ((), ()))
TN = (((0,), (0,)), ((), ()))


def mm(a, b, dims):
    return lax.dot_general(a, b, dims, preferred_element_type=jnp.float32)


def layer_kernel(
    chips, rows, scale,
    patch_hbm, token_hbm, cot_hbm, hidden_hbm, present_hbm, rdec_hbm, cdec_hbm, w_hbm, wout_hbm,
    pg_ref, out_ref,
    patch_ref, token_ref, cot_ref, hidden_ref, present_ref, rdec_ref, cdec_ref, in_sem,
    xs, gs, rd, cd, xb, gb, db, wa, wb, wout, u_s, z_s, gn_s, bc_s, normed_s, y_s, mat_s, dec_s, gp, grow, gcol,
    xsend, wgo, xr, zs, zr,
    x_send, x_recv, g_send, g_recv, d_send, d_recv, w_sem, l_sem,
    gp_send, gp_recv, xr_send, xr_recv, z_send, z_recv,
):
    k, c = lax.axis_index("gcol"), lax.axis_index("grow")
    depth = chips // 2
    zi, xi = k // 2, lax.rem(k, 2)
    cols, feat = xs.shape[1], xs.shape[2]
    toks = chips * cols
    half, part = wout.shape[1], wa.shape[1]
    total = 2 * chips

    load_w = pltpu.make_async_copy(w_hbm, wa, l_sem.at[0])
    load_o = pltpu.make_async_copy(wout_hbm, wout, l_sem.at[1])
    loads = [
        pltpu.make_async_copy(src, dst, in_sem.at[i])
        for i, (src, dst) in enumerate(
            (
                (hidden_hbm, hidden_ref), (present_hbm, present_ref), (token_hbm, token_ref),
                (patch_hbm, patch_ref), (rdec_hbm, rdec_ref), (cdec_hbm, cdec_ref), (cot_hbm, cot_ref),
            )
        )
    ]
    for copy in loads:
        copy.start()
    load_w.start()
    load_o.start()

    me = 2 * k + c
    barrier = pltpu.get_barrier_semaphore()
    for d in range(1, total):
        to = lax.rem(me + d, total)
        pl.semaphore_signal(
            barrier, inc=1, device_id={"gcol": to // 2, "grow": lax.rem(to, 2)}, device_id_type=MESH
        )

    def remote(src, dst, s, r, chip, core):
        return pltpu.make_async_remote_copy(
            src_ref=src, dst_ref=dst, send_sem=s, recv_sem=r,
            device_id={"gcol": chip, "grow": core}, device_id_type=MESH,
        )

    for copy in loads[:-1]:
        copy.wait()
    square = (cols, cols)
    eye = lax.broadcasted_iota(jnp.int32, square, 0) == lax.broadcasted_iota(jnp.int32, square, 1)
    eye = eye.astype(jnp.float32)
    hidden_t = mm(eye, hidden_ref[...].astype(jnp.float32), NT)
    present_t = mm(eye, present_ref[...].astype(jnp.float32), NT)
    token = token_ref[...].reshape(1, feat).astype(jnp.float32)
    for i in range(rows):
        hidden, present = hidden_t[:, i : i + 1], present_t[:, i : i + 1]
        chosen = jnp.where(hidden > 0.5, token, patch_ref[i].astype(jnp.float32))
        xs[i] = (chosen * present).astype(jnp.bfloat16)
        rd[i] = rdec_ref[:, i, :]
        cd[i] = cdec_ref[:, i, :]

    streams = (
        (xs, xs, xb, x_send, x_recv),
        (rd, cd, db, d_send, d_recv),
        (gs, gs, gb, g_send, g_recv),
    )

    def row_out(stream, i):
        row_src, _, dst, s, r = stream
        return remote(row_src.at[i], dst.at[k], s.at[i], r.at[k], rows * c + i, 0)

    def col_out(stream):
        _, col_src, dst, s, r = stream
        return remote(col_src, dst.at[pl.ds(0, rows)], s.at[rows], r.at[chips], k, 1)

    def row_in(stream, src):
        row_src, _, dst, s, r = stream
        return remote(row_src.at[0], dst.at[src], s.at[0], r.at[src], k, 1 - c)

    def col_in(stream):
        _, col_src, dst, s, r = stream
        return remote(col_src, dst.at[pl.ds(0, rows)], s.at[rows], r.at[chips], k, 1 - c)

    def launch(stream):
        for i in range(rows):

            @pl.when(jnp.logical_or(c == 1, k != i))
            def _():
                row_out(stream, i).start()

        @pl.when(c == 0)
        def _():
            col_out(stream).start()

    def arrive(stream):
        @pl.when(c == 0)
        def _():
            for d in range(1, chips):
                row_in(stream, lax.rem(k + d, chips)).wait_recv()

            @pl.when(k >= rows)
            def _():
                row_in(stream, k).wait_recv()

        @pl.when(c == 1)
        def _():
            col_in(stream).wait_recv()

    def drain(stream):
        for i in range(rows):

            @pl.when(jnp.logical_or(c == 1, k != i))
            def _():
                row_out(stream, i).wait_send()

        @pl.when(c == 0)
        def _():
            col_out(stream).wait_send()

    pl.semaphore_wait(barrier, total - 1)
    weights = remote(w_hbm, wb, w_sem.at[0], w_sem.at[1], k, 1 - c)
    launch(streams[0])
    launch(streams[1])
    weights.start()
    loads[-1].wait()
    for i in range(rows):
        gs[i] = (cot_ref[i].astype(jnp.float32) * hidden_t[:, i : i + 1]).astype(jnp.bfloat16)
    launch(streams[2])

    for row_src, col_src, dst, _, _ in streams:

        @pl.when(c == 1)
        def _():
            dst[pl.ds(rows, rows)] = col_src[...]

        for i in range(rows):

            @pl.when(jnp.logical_and(c == 0, k == i))
            def _():
                dst[i] = row_src[i]

    t_at = lax.broadcasted_iota(jnp.int32, (toks, toks), 0)
    k_at = lax.broadcasted_iota(jnp.int32, (toks, toks), 1)
    step = jnp.where(c == 0, 1, cols)
    mask = jnp.logical_and(t_at >= k_at, lax.rem(t_at, step) == lax.rem(k_at, step))
    low = lax.broadcasted_iota(jnp.int32, (toks, 128), 1) < N

    arrive(streams[1])
    ones = mask.astype(jnp.float32)
    dec = jnp.concatenate([db[i] for i in range(chips)], axis=1)
    run_s = lax.dot_general(ones, dec, NT, precision=PRECISE, preferred_element_type=jnp.float32)
    run_l = lax.dot_general(dec, ones, NT, precision=PRECISE, preferred_element_type=jnp.float32)
    heads = dec.shape[0]
    for h in range(heads):
        gap = run_s[:, h : h + 1] - run_l[h : h + 1, :]
        dec_s[h] = jnp.where(mask, jnp.exp(jnp.minimum(gap, 0.0)), 0.0)

    load_w.wait()
    arrive(streams[0])
    mine, rest = pl.multiple_of(c * part, part), pl.multiple_of((1 - c) * part, part)
    own = xb[:, :, pl.ds(mine, part)].reshape(toks, part)
    oth = xb[:, :, pl.ds(rest, part)].reshape(toks, part)
    pieces = ((u_s, c * half, half), (z_s, 2 * half + c * half, half), (bc_s, 4 * half + c * 2 * N, 2 * N))
    partial = [
        mm(own, wa[pl.ds(pl.multiple_of(start, 128), size), :], NT) for _, start, size in pieces
    ]
    weights.wait_recv()
    for (dst, start, size), first in zip(pieces, partial):
        second = mm(oth, wb[pl.ds(pl.multiple_of(start, 128), size), :], NT)
        dst[...] = (first + second).astype(jnp.bfloat16)

    b_bf, c_bf = bc_s[:, :N], bc_s[:, N:]
    scores = mm(c_bf, b_bf, NT)

    def per_head(x):
        first = jnp.sum(jnp.where(low, x, 0.0), axis=1, keepdims=True)
        second = jnp.sum(jnp.where(low, 0.0, x), axis=1, keepdims=True)
        return jnp.where(low, first, second) * (1.0 / N)

    def norm(p):
        cols_p = slice(p * 128, (p + 1) * 128)
        z = z_s[:, cols_p].astype(jnp.float32)
        sig_z = 1.0 / (1.0 + jnp.exp(-z))
        y = y_s[:, cols_p]
        gated = y * (z * sig_z)
        inv = lax.rsqrt(per_head(gated * gated) + EPSILON)
        return cols_p, z, sig_z, y, inv, gated * inv

    for p in range(half // 128):
        cols_p = slice(p * 128, (p + 1) * 128)
        u = u_s[:, cols_p].astype(jnp.float32)
        val_bf = (u / (1.0 + jnp.exp(-u))).astype(jnp.bfloat16)
        for h in (2 * p, 2 * p + 1):
            mat_s[h] = (dec_s[h] * scores).astype(jnp.bfloat16)
        y_s[:, cols_p] = jnp.where(
            low, mm(mat_s[2 * p], val_bf, NN), mm(mat_s[2 * p + 1], val_bf, NN)
        )
        normed_s[:, cols_p] = norm(p)[-1].astype(jnp.bfloat16)

    load_o.wait()
    arrive(streams[2])

    def weight_block(chip):
        at = pl.ds(pl.multiple_of(chip * 128, 128), 128)
        return mm(gb[:, :, at].reshape(toks, 128), normed_s[...], TN)

    def across(q):
        return remote(xsend.at[q], xr.at[q], xr_send.at[q], xr_recv.at[q], 2 * zi + 1 - xi, c)

    order = [lax.rem(zi + 1 + j, depth) for j in range(depth)]
    for q in order:
        xsend[q] = weight_block(2 * q + 1 - xi).astype(jnp.bfloat16)
        across(q).start()

    def along(q, core):
        return remote(
            zs.at[q, core], zr.at[zi, c], z_send.at[2 * q + core], z_recv.at[2 * zi + c], 2 * q + xi, core
        )

    def forward(q):
        across(q).wait_recv()
        both = wgo[q] + xr[q].astype(jnp.float32)
        wgo[q] = both
        zs[q] = both.astype(jnp.bfloat16).reshape(2, both.shape[0] // 2, both.shape[1])

    def forward_far(q):
        forward(q)
        for core in range(2):
            along(q, core).start()

    grads = gb[...].reshape(toks, feat)
    gn_s[...] = mm(grads, wout[...], NN).astype(jnp.bfloat16)
    d_scores = jnp.zeros((toks, toks), jnp.float32)
    for p in range(half // 128):
        cols_p, z, sig_z, y, inv, normed = norm(p)
        u = u_s[:, cols_p].astype(jnp.float32)
        sig_u = 1.0 / (1.0 + jnp.exp(-u))
        val_bf = (u * sig_u).astype(jnp.bfloat16)
        gn = gn_s[:, cols_p].astype(jnp.float32)
        gg = inv * (gn - normed * per_head(gn * normed))
        dy = gg * (z * sig_z)
        dz = gg * y * (sig_z * (1.0 + z * (1.0 - sig_z)))
        dy_bf = dy.astype(jnp.bfloat16)
        dv = jnp.where(low, mm(mat_s[2 * p], dy_bf, TN), mm(mat_s[2 * p + 1], dy_bf, TN))
        du = dv * (sig_u * (1.0 + u * (1.0 - sig_u)))
        gp[:, :, cols_p] = du.astype(jnp.bfloat16).reshape(chips, cols, 128)
        gp[:, :, half + p * 128 : half + (p + 1) * 128] = dz.astype(jnp.bfloat16).reshape(
            chips, cols, 128
        )
        zero = jnp.zeros_like(dy)
        d_scores += dec_s[2 * p] * mm(jnp.where(low, dy, zero).astype(jnp.bfloat16), val_bf, NT)
        d_scores += dec_s[2 * p + 1] * mm(jnp.where(low, zero, dy).astype(jnp.bfloat16), val_bf, NT)
        if p < depth:
            wgo[order[p]] = weight_block(2 * order[p] + xi)
        if p == 2:
            forward_far(order[0])
    ds_bf = d_scores.astype(jnp.bfloat16)
    d_bc = jnp.concatenate([mm(ds_bf, c_bf, TN), mm(ds_bf, b_bf, NN)], axis=1)
    gp[:, :, 2 * half :] = d_bc.astype(jnp.bfloat16).reshape(chips, cols, 2 * N)

    home, slot = k // rows, lax.rem(k, rows)

    def row_back(chip):
        return remote(gp.at[chip], grow.at[slot], gp_send.at[chip], gp_recv.at[slot], chip, home)

    def col_back(core):
        lo = pl.ds(0, rows)
        return remote(gp.at[lo], gcol, gp_send.at[chips], gp_recv.at[rows], k, core)

    @pl.when(c == 0)
    def _():
        for d in range(1, chips):
            row_back(lax.rem(k + d, chips)).start()

        @pl.when(home == 1)
        def _():
            row_back(k).start()

        for i in range(rows):

            @pl.when(k == i)
            def _():
                grow[i] = gp[i]

    @pl.when(c == 1)
    def _():
        col_back(0).start()
        gcol[...] = gp[pl.ds(rows, rows)]

    def back_project(src, g, w_ref):
        flat = src[...].reshape(rows * cols, 2 * half + 2 * N)
        acc = mm(flat[:, :half], w_ref[g * half : (g + 1) * half, :], NN)
        acc += mm(flat[:, half : 2 * half], w_ref[(2 + g) * half : (3 + g) * half, :], NN)
        at = 4 * half + g * 2 * N
        return acc + mm(flat[:, 2 * half :], w_ref[at : at + 2 * N, :], NN)

    for q in order[half // 128 :]:
        wgo[q] = weight_block(2 * q + xi)
    forward_far(order[1])

    @pl.when(c == 0)
    def _():
        col_back(1).wait_recv()

    col_part = [back_project(gcol, 1, w_ref) for w_ref in (wa, wb)]
    for q in order[2:-1]:
        forward_far(q)
    forward(zi)
    along(zi, 1 - c).start()

    for i in range(rows):

        @pl.when(jnp.logical_or(c == 1, k != i))
        def _():
            remote(gp.at[0], grow.at[i], gp_send.at[0], gp_recv.at[i], k, 1 - c).wait_recv()

    for w_ref, at, first in ((wa, mine, col_part[0]), (wb, rest, col_part[1])):
        acc = (first + back_project(grow, 0, w_ref)).reshape(rows, cols, part)
        for i in range(rows):
            keep = present_t[:, i : i + 1] * (1.0 - hidden_t[:, i : i + 1])
            pg_ref[i, :, pl.ds(at, part)] = (acc[i] * keep).astype(pg_ref.dtype)

    for q in order[:-1]:
        for core in range(2):
            remote(zs.at[0, 0], zr.at[q, core], z_send.at[0], z_recv.at[2 * q + core], k, 1 - c).wait_recv()
    remote(zs.at[0, 0], zr.at[zi, 1 - c], z_send.at[0], z_recv.at[2 * zi + 1 - c], k, 1 - c).wait_recv()
    zr[zi, c] = zs[zi, c]
    for core in range(2):
        acc = zr[0, core].astype(jnp.float32)
        for q in range(1, depth):
            acc += zr[q, core].astype(jnp.float32)
        out_ref[:, core * half : (core + 1) * half] = acc * scale

    for stream in streams:
        drain(stream)
    weights.wait_send()
    for q in order:
        across(q).wait_send()
    for q in order[:-1]:
        for core in range(2):
            along(q, core).wait_send()
    along(zi, 1 - c).wait_send()

    @pl.when(c == 0)
    def _():
        for d in range(1, chips):
            row_back(lax.rem(k + d, chips)).wait_send()

        @pl.when(home == 1)
        def _():
            row_back(k).wait_send()

    @pl.when(c == 1)
    def _():
        col_back(0).wait_send()


def owned(
    patches, mask_token, masked, tissue, in_weight, out_weight, row_decay, col_decay, cotangent
):
    rows, cols, feat = patches.shape
    chips = lax.axis_size("gcol")
    toks, heads = chips * cols, row_decay.shape[0]
    half, part = out_weight.shape[1], in_weight.shape[1]
    width = 2 * half + 2 * N
    slab = feat // (2 * chips)
    depth = chips // 2
    bf, fl = jnp.bfloat16, jnp.float32
    vmem, dma = pltpu.VMEM, pltpu.SemaphoreType.DMA
    in_vmem, anywhere = pl.BlockSpec(memory_space=pltpu.VMEM), pl.BlockSpec(memory_space=pltpu.HBM)
    scale = 1.0 / math.sqrt(2 * rows * cols * chips)
    return pl.pallas_call(
        functools.partial(layer_kernel, chips, rows, scale),
        name="layer",
        out_shape=(
            jax.ShapeDtypeStruct(patches.shape, bf),
            jax.ShapeDtypeStruct((slab, 2 * half), fl),
        ),
        in_specs=[anywhere] * 9,
        out_specs=(in_vmem, in_vmem),
        scratch_shapes=[
            vmem(patches.shape, bf), vmem(mask_token.shape, bf), vmem(patches.shape, bf),
            vmem(masked.shape, masked.dtype), vmem(tissue.shape, tissue.dtype),
            vmem(row_decay.shape, fl), vmem(col_decay.shape, fl), dma((7,)),
            vmem((rows, cols, feat), bf), vmem((rows, cols, feat), bf),
            vmem((rows, heads, cols), fl), vmem((rows, heads, cols), fl),
            vmem((chips, cols, feat), bf), vmem((chips, cols, feat), bf), vmem((chips, heads, cols), fl),
            vmem(in_weight.shape, bf), vmem(in_weight.shape, bf), vmem(out_weight.shape, bf),
            vmem((toks, half), bf), vmem((toks, half), bf), vmem((toks, half), bf),
            vmem((toks, 2 * N), bf), vmem((toks, half), bf), vmem((toks, half), fl),
            vmem((heads, toks, toks), bf), vmem((heads, toks, toks), fl),
            vmem((chips, cols, width), bf), vmem((rows, cols, width), bf), vmem((rows, cols, width), bf),
            vmem((depth, 2 * slab, half), bf), vmem((depth, 2 * slab, half), fl),
            vmem((depth, 2 * slab, half), bf), vmem((depth, 2, slab, half), bf),
            vmem((depth, 2, slab, half), bf),
            dma((rows + 1,)), dma((chips + 1,)), dma((rows + 1,)), dma((chips + 1,)),
            dma((rows + 1,)), dma((chips + 1,)), dma((2,)), dma((2,)),
            dma((chips + 1,)), dma((rows + 1,)), dma((depth,)), dma((depth,)),
            dma((2 * depth,)), dma((2 * depth,)),
        ],
        compiler_params=pltpu.CompilerParams(
            collective_id=0, has_side_effects=True, vmem_limit_bytes=60 << 20
        ),
    )(
        patches, mask_token, cotangent, masked, tissue, row_decay, col_decay,
        in_weight, out_weight,
    )


def body(*args):
    rows = args[0].shape[0]
    if lax.axis_size("grow") == 2 and lax.axis_size("gcol") == 2 * rows:
        return owned(*args)
    return shards(*args)


def solution(mesh):
    return jax.shard_map(
        body,
        mesh=mesh,
        in_specs=(
            P(("groups", "grow"), "gcol", None),
            P(),
            P(("groups", "grow"), "gcol"),
            P(("groups", "grow"), "gcol"),
            P(None, "grow"),
            P(None, "grow"),
            P(None, ("groups", "grow"), "gcol"),
            P(None, ("groups", "grow"), "gcol"),
            P(("groups", "grow"), "gcol", None),
        ),
        out_specs=(P(("groups", "grow"), "gcol", None), P(("groups", "gcol", "grow"), None)),
        check_vma=False,
    )
```

```python
import functools
import math

import jax
import jax.numpy as jnp
from jax import lax
from jax.experimental import pallas as pl
from jax.experimental.pallas import tpu as pltpu
from jax.sharding import PartitionSpec as P

E = 1024
HEADS = 16
N = 64


EPSILON = 1e-05
PRECISE = lax.Precision.HIGHEST


def prefix(value, axis, join, neutral):
    count, mine = (lax.axis_size(axis), lax.axis_index(axis))
    pieces = jax.tree.map(lambda part: lax.all_gather(part, axis), value)
    so_far = jax.tree.map(
        lambda part, zero: jnp.full_like(part, 0) + jnp.asarray(zero, part.dtype), value, neutral
    )

    def prefix_hop(position, so_far):
        longer = join(so_far, jax.tree.map(lambda part: part[position], pieces))
        return jax.tree.map(lambda new, old: jnp.where(position < mine, new, old), longer, so_far)

    return lax.fori_loop(0, count - 1, prefix_hop, so_far)


def carried_in(shard, axis, combine, identity):
    length, position = (lax.axis_size(axis), lax.axis_index(axis))
    everything = jax.tree.map(
        lambda part, kind: lax.all_gather(part.astype(kind), axis),
        shard,
        jax.tree.map(lambda a: jnp.bfloat16 if a.dtype == jnp.float32 else a.dtype, shard),
    )
    start = jax.tree.map(
        lambda part, zero: jnp.broadcast_to(jnp.asarray(zero, part.dtype), part.shape),
        shard,
        identity,
    )

    def carried_hop(k, before):
        at = length - 1 - k
        reached = at > position
        new = combine(
            before, jax.tree.map(lambda part, own: part[at].astype(own.dtype), everything, shard)
        )
        return jax.tree.map(lambda a, b: jnp.where(reached, a, b), new, before)

    return lax.fori_loop(0, length, carried_hop, start)


def shortened(shard):

    def short(part):
        return part.astype(jnp.bfloat16) if part.dtype == jnp.float32 else part

    return jax.tree.map(short, shard)


def silu_grad(pre_act):
    sigmoid_v = jax.nn.sigmoid(pre_act)
    return sigmoid_v * (1.0 + pre_act * (1.0 - sigmoid_v))


def per_channel(head_part, channels):
    return jnp.repeat(head_part, channels // head_part.shape[-1], axis=-1)


def line_form(head_lines, channels):
    return per_channel(head_lines.transpose(1, 2, 0), channels)


def carry_on(log_lines, state):
    return per_channel(jnp.exp(log_lines), state.shape[2])[:, None, :] * state


def prepare(log_decay):
    length = log_decay.shape[2]
    running = jnp.cumsum(log_decay, axis=2)
    whole_log = running[:, :, -1]
    causal = jnp.arange(length)[:, None] >= jnp.arange(length)[None, :]
    log_gaps = running[:, :, :, None] - running[:, :, None, :]
    decay_mat = jnp.where(causal, jnp.exp(jnp.where(causal, log_gaps, 0.0)), 0.0)
    return (running, whole_log, decay_mat)


def chain_link(earlier, later):
    return (earlier[0] + later[0], carry_on(later[0], earlier[1]) + later[1])


def split_heads(lines, head_count):
    line_count, length, channels = lines.shape
    return lines.reshape(line_count, length, head_count, channels // head_count)


def local_summary(inputs, key_vecs, prepared):
    running, whole_log, decay_mat = prepared
    to_end = line_form(jnp.exp(whole_log[:, :, None] - running), inputs.shape[2])
    fresh = jnp.einsum("ltc,ltn->lnc", inputs * to_end, key_vecs, precision=PRECISE)
    return (whole_log.T, fresh)


def local_return(query_vecs, prepared, upstream):
    running, whole_log, decay_mat = prepared
    from_start = line_form(jnp.exp(running), upstream.shape[2])
    backward = jnp.einsum("ltc,ltn->lnc", upstream * from_start, query_vecs, precision=PRECISE)
    return (whole_log.T, backward)


def local_outputs(inputs, key_vecs, query_vecs, prepared, incoming):
    running, whole_log, decay_mat = prepared
    head_count = decay_mat.shape[0]
    line_count, length, channels = inputs.shape
    scores = jnp.einsum("ltn,lkn->ltk", query_vecs, key_vecs, precision=PRECISE)
    within = jnp.einsum(
        "gltk,lkgp->ltgp",
        decay_mat * scores[None],
        split_heads(inputs, head_count),
        precision=PRECISE,
    )
    within = within.reshape(line_count, length, channels)
    carried = jnp.einsum("ltn,lnc->ltc", query_vecs, incoming, precision=PRECISE)
    return within + carried * line_form(jnp.exp(running), channels)


def local_grads(inputs, key_vecs, query_vecs, prepared, incoming, returning, upstream):
    running, whole_log, decay_mat = prepared
    head_count = decay_mat.shape[0]
    line_count, length, channels = inputs.shape
    from_start = line_form(jnp.exp(running), channels)
    to_end = line_form(jnp.exp(whole_log[:, :, None] - running), channels)
    scores = jnp.einsum("ltn,lkn->ltk", query_vecs, key_vecs, precision=PRECISE)
    heads_up = split_heads(upstream, head_count)
    heads_in = split_heads(inputs, head_count)
    grad_inputs = jnp.einsum(
        "gltk,ltgp->lkgp", decay_mat * scores[None], heads_up, precision=PRECISE
    ).reshape(line_count, length, channels)
    grad_inputs = (
        grad_inputs + jnp.einsum("lnc,lkn->lkc", returning, key_vecs, precision=PRECISE) * to_end
    )
    mixed = jnp.einsum("ltgp,lkgp->gltk", heads_up, heads_in, precision=PRECISE) * decay_mat
    grad_keys = jnp.einsum("gltk,ltn->lkn", mixed, query_vecs, precision=PRECISE)
    grad_keys = grad_keys + jnp.einsum(
        "lkc,lnc->lkn", inputs * to_end, returning, precision=PRECISE
    )
    grad_queries = jnp.einsum("gltk,lkn->ltn", mixed, key_vecs, precision=PRECISE)
    grad_queries = grad_queries + jnp.einsum(
        "ltc,lnc->ltn", upstream * from_start, incoming, precision=PRECISE
    )
    return (grad_inputs, grad_keys, grad_queries)


def shards(
    patches, mask_token, masked, tissue, in_weight, out_weight, row_decay, col_decay, cotangent
):
    grid_rows, grid_cols, feat_width = patches.shape
    tok_count = grid_rows * grid_cols
    chosen = (masked == 1)[:, :, None]
    present = tissue.astype(jnp.bfloat16)[:, :, None]
    model_in = jnp.where(chosen, mask_token[None, None, :], patches) * present
    flat_in = model_in.reshape(tok_count, feat_width)
    inner_width = E
    half_width = inner_width // 2
    state_size = N
    number_of_heads = HEADS // 2
    offset = 2 * inner_width
    full_in, full_out = (
        lax.all_gather(in_weight, "grow", axis=1, tiled=True),
        lax.all_gather(out_weight, "grow", axis=1, tiled=True),
    )
    projected = lax.dot_general(
        flat_in, full_in, (((1,), (1,)), ((), ())), preferred_element_type=jnp.float32
    )
    proj_bf = projected.astype(jnp.bfloat16)
    pre_values = proj_bf[:, :inner_width].astype(jnp.float32)
    gate_pre = proj_bf[:, inner_width:offset].astype(jnp.float32)
    key_rows = (
        proj_bf[:, offset : offset + state_size]
        .astype(jnp.float32)
        .reshape(grid_rows, grid_cols, state_size)
    )
    query_rows = (
        proj_bf[:, offset + state_size : offset + 2 * state_size]
        .astype(jnp.float32)
        .reshape(grid_rows, grid_cols, state_size)
    )
    key_cols = (
        proj_bf[:, offset + 2 * state_size : offset + 3 * state_size]
        .astype(jnp.float32)
        .reshape(grid_rows, grid_cols, state_size)
        .transpose(1, 0, 2)
    )
    query_cols = (
        proj_bf[:, offset + 3 * state_size : offset + 4 * state_size]
        .astype(jnp.float32)
        .reshape(grid_rows, grid_cols, state_size)
        .transpose(1, 0, 2)
    )
    values = jax.nn.silu(pre_values)
    row_inputs = values[:, :half_width].reshape(grid_rows, grid_cols, half_width)
    col_inputs = values[:, half_width:].reshape(grid_rows, grid_cols, half_width).transpose(1, 0, 2)
    row_prep = prepare(row_decay)
    col_prep = prepare(col_decay.transpose(0, 2, 1))
    row_zero = (
        jnp.zeros((grid_rows, number_of_heads), jnp.float32),
        jnp.zeros((grid_rows, state_size, half_width), jnp.float32),
    )
    col_zero = (
        jnp.zeros((grid_cols, number_of_heads), jnp.float32),
        jnp.zeros((grid_cols, state_size, half_width), jnp.float32),
    )
    row_entry = prefix(local_summary(row_inputs, key_rows, row_prep), "gcol", chain_link, row_zero)[
        1
    ]
    grow_size = lax.axis_size("grow")
    my_block = lax.axis_index("grow")
    parts_in, parts_key, parts_log = (
        lax.all_gather(
            proj_bf[:, half_width:inner_width].reshape(grid_rows, grid_cols, half_width),
            "grow",
            axis=0,
            tiled=True,
        ),
        lax.all_gather(
            proj_bf[:, offset + 2 * state_size : offset + 3 * state_size].reshape(
                grid_rows, grid_cols, state_size
            ),
            "grow",
            axis=0,
            tiled=True,
        ),
        lax.all_gather(
            col_decay.transpose(1, 0, 2).astype(jnp.bfloat16), "grow", axis=0, tiled=True
        ).astype(jnp.float32),
    )
    col_entry = col_zero[1]
    for block_idx in range(grow_size):
        lower_row = block_idx * grid_rows
        piece_in = jax.nn.silu(
            parts_in[lower_row : lower_row + grid_rows].astype(jnp.float32)
        ).transpose(1, 0, 2)
        piece_keys = (
            parts_key[lower_row : lower_row + grid_rows].astype(jnp.float32).transpose(1, 0, 2)
        )
        piece_log = parts_log[lower_row : lower_row + grid_rows].transpose(1, 2, 0)
        whole_log, piece_state = local_summary(piece_in, piece_keys, prepare(piece_log))
        moved = carry_on(whole_log, col_entry) + piece_state
        col_entry = jnp.where(block_idx < my_block, moved, col_entry)
    row_out = local_outputs(row_inputs, key_rows, query_rows, row_prep, row_entry)
    col_out = local_outputs(col_inputs, key_cols, query_cols, col_prep, col_entry).transpose(
        1, 0, 2
    )
    mixed = jnp.concatenate(
        [row_out.reshape(tok_count, half_width), col_out.reshape(tok_count, half_width)], axis=1
    )
    gate_act = jax.nn.silu(gate_pre)
    head_size = inner_width // HEADS
    gated = (mixed * gate_act).reshape(tok_count, HEADS, head_size)
    inv_rms = lax.rsqrt(jnp.mean(gated * gated, axis=2, keepdims=True) + EPSILON)
    normed = gated * inv_rms
    normed_bf = normed.reshape(tok_count, inner_width).astype(jnp.bfloat16)
    grad_out = (cotangent * masked.astype(jnp.bfloat16)[:, :, None]).reshape(tok_count, feat_width)
    total_patches = tok_count * lax.axis_size("gcol") * lax.axis_size("grow")
    weight_sum = lax.psum_scatter(
        lax.dot_general(
            grad_out, normed_bf, (((0,), (0,)), ((), ())), preferred_element_type=jnp.float32
        ),
        ("gcol", "grow"),
        scatter_dimension=0,
        tiled=True,
    )
    out_weight_grad = weight_sum * (1.0 / math.sqrt(total_patches))
    grad_normed_bf = jnp.dot(grad_out, full_out, preferred_element_type=jnp.float32).astype(
        jnp.bfloat16
    )
    grad_normed = lax.optimization_barrier(grad_normed_bf).astype(jnp.float32)
    grad_normed = grad_normed.reshape(tok_count, HEADS, head_size)
    grad_gated = inv_rms * (
        grad_normed - normed * jnp.mean(grad_normed * normed, axis=2, keepdims=True)
    )
    grad_gated = grad_gated.reshape(tok_count, inner_width)
    grad_mixed = grad_gated * gate_act
    grad_gate = grad_gated * mixed * silu_grad(gate_pre)
    row_up = grad_mixed[:, :half_width].reshape(grid_rows, grid_cols, half_width)
    col_up = grad_mixed[:, half_width:].reshape(grid_rows, grid_cols, half_width).transpose(1, 0, 2)
    row_exit = carried_in(local_return(query_rows, row_prep, row_up), "gcol", chain_link, row_zero)[
        1
    ]
    parts_up, parts_query = (
        lax.all_gather(
            shortened(grad_mixed[:, half_width:].reshape(grid_rows, grid_cols, half_width)),
            "grow",
            axis=0,
            tiled=True,
        ),
        lax.all_gather(
            proj_bf[:, offset + 3 * state_size : offset + 4 * state_size].reshape(
                grid_rows, grid_cols, state_size
            ),
            "grow",
            axis=0,
            tiled=True,
        ),
    )
    col_exit = col_zero[1]
    for block_idx in reversed(range(grow_size)):
        lower_row = block_idx * grid_rows
        piece_up = parts_up[lower_row : lower_row + grid_rows].transpose(1, 0, 2)
        piece_queries = (
            parts_query[lower_row : lower_row + grid_rows].astype(jnp.float32).transpose(1, 0, 2)
        )
        piece_log = parts_log[lower_row : lower_row + grid_rows].transpose(1, 2, 0)
        whole_log, piece_back = local_return(piece_queries, prepare(piece_log), piece_up)
        moved = carry_on(whole_log, col_exit) + piece_back
        col_exit = jnp.where(block_idx > my_block, moved, col_exit)
    grad_row_in, grad_row_key, grad_row_query = local_grads(
        row_inputs, key_rows, query_rows, row_prep, row_entry, row_exit, row_up
    )
    grad_col_in, grad_col_key, grad_col_query = local_grads(
        col_inputs, key_cols, query_cols, col_prep, col_entry, col_exit, col_up
    )
    grad_values = jnp.concatenate(
        [
            grad_row_in.reshape(tok_count, half_width),
            grad_col_in.transpose(1, 0, 2).reshape(tok_count, half_width),
        ],
        axis=1,
    )
    grad_proj = jnp.concatenate(
        [
            grad_values * silu_grad(pre_values),
            grad_gate,
            grad_row_key.reshape(tok_count, state_size),
            grad_row_query.reshape(tok_count, state_size),
            grad_col_key.transpose(1, 0, 2).reshape(tok_count, state_size),
            grad_col_query.transpose(1, 0, 2).reshape(tok_count, state_size),
        ],
        axis=1,
    ).astype(jnp.bfloat16)
    keep_mask = present * (1 - masked).astype(jnp.bfloat16)[:, :, None]
    grad_model_in = jnp.dot(grad_proj, full_in, preferred_element_type=jnp.float32).reshape(
        grid_rows, grid_cols, feat_width
    )
    patch_grad = (grad_model_in * keep_mask).astype(jnp.bfloat16)
    return (patch_grad, out_weight_grad)


MESH = pl.DeviceIdType.MESH
NT = (((1,), (1,)), ((), ()))
NN = (((1,), (0,)), ((), ()))
TN = (((0,), (0,)), ((), ()))


def mm(a, b, dims):
    return lax.dot_general(a, b, dims, preferred_element_type=jnp.float32)


def layer_kernel(
    chips, rows, scale,
    patch_hbm, token_hbm, cot_hbm, hidden_hbm, present_hbm, rdec_hbm, cdec_hbm, w_hbm, wout_hbm,
    pg_ref, out_ref,
    patch_ref, token_ref, cot_ref, hidden_ref, present_ref, rdec_ref, cdec_ref, in_sem,
    xs, gs, rd, cd, xb, gb, db, wa, wb, wout, u_s, z_s, gn_s, bc_s, normed_s, y_s, mat_s, dec_s, gp, grow, gcol,
    xsend, wgo, xr, zs, zr,
    x_send, x_recv, g_send, g_recv, d_send, d_recv, w_sem, l_sem,
    gp_send, gp_recv, xr_send, xr_recv, z_send, z_recv,
):
    k, c = lax.axis_index("gcol"), lax.axis_index("grow")
    depth = chips // 2
    zi, xi = k // 2, lax.rem(k, 2)
    cols, feat = xs.shape[1], xs.shape[2]
    toks = chips * cols
    half, part = wout.shape[1], wa.shape[1]
    total = 2 * chips

    load_w = pltpu.make_async_copy(w_hbm, wa, l_sem.at[0])
    load_o = pltpu.make_async_copy(wout_hbm, wout, l_sem.at[1])
    loads = [
        pltpu.make_async_copy(src, dst, in_sem.at[i])
        for i, (src, dst) in enumerate(
            (
                (hidden_hbm, hidden_ref), (present_hbm, present_ref), (token_hbm, token_ref),
                (patch_hbm, patch_ref), (rdec_hbm, rdec_ref), (cdec_hbm, cdec_ref), (cot_hbm, cot_ref),
            )
        )
    ]
    for copy in loads:
        copy.start()
    load_w.start()
    load_o.start()

    me = 2 * k + c
    barrier = pltpu.get_barrier_semaphore()
    for d in range(1, total):
        to = lax.rem(me + d, total)
        pl.semaphore_signal(
            barrier, inc=1, device_id={"gcol": to // 2, "grow": lax.rem(to, 2)}, device_id_type=MESH
        )

    def remote(src, dst, s, r, chip, core):
        return pltpu.make_async_remote_copy(
            src_ref=src, dst_ref=dst, send_sem=s, recv_sem=r,
            device_id={"gcol": chip, "grow": core}, device_id_type=MESH,
        )

    for copy in loads[:-1]:
        copy.wait()
    square = (cols, cols)
    eye = lax.broadcasted_iota(jnp.int32, square, 0) == lax.broadcasted_iota(jnp.int32, square, 1)
    eye = eye.astype(jnp.float32)
    hidden_t = mm(eye, hidden_ref[...].astype(jnp.float32), NT)
    present_t = mm(eye, present_ref[...].astype(jnp.float32), NT)
    token = token_ref[...].reshape(1, feat).astype(jnp.float32)
    for i in range(rows):
        hidden, present = hidden_t[:, i : i + 1], present_t[:, i : i + 1]
        chosen = jnp.where(hidden > 0.5, token, patch_ref[i].astype(jnp.float32))
        xs[i] = (chosen * present).astype(jnp.bfloat16)
        rd[i] = rdec_ref[:, i, :]
        cd[i] = cdec_ref[:, i, :]

    streams = (
        (xs, xs, xb, x_send, x_recv),
        (rd, cd, db, d_send, d_recv),
        (gs, gs, gb, g_send, g_recv),
    )

    def row_out(stream, i):
        row_src, _, dst, s, r = stream
        return remote(row_src.at[i], dst.at[k], s.at[i], r.at[k], rows * c + i, 0)

    def col_out(stream):
        _, col_src, dst, s, r = stream
        return remote(col_src, dst.at[pl.ds(0, rows)], s.at[rows], r.at[chips], k, 1)

    def row_in(stream, src):
        row_src, _, dst, s, r = stream
        return remote(row_src.at[0], dst.at[src], s.at[0], r.at[src], k, 1 - c)

    def col_in(stream):
        _, col_src, dst, s, r = stream
        return remote(col_src, dst.at[pl.ds(0, rows)], s.at[rows], r.at[chips], k, 1 - c)

    def launch(stream):
        for i in range(rows):

            @pl.when(jnp.logical_or(c == 1, k != i))
            def _():
                row_out(stream, i).start()

        @pl.when(c == 0)
        def _():
            col_out(stream).start()

    def arrive(stream):
        @pl.when(c == 0)
        def _():
            for d in range(1, chips):
                row_in(stream, lax.rem(k + d, chips)).wait_recv()

            @pl.when(k >= rows)
            def _():
                row_in(stream, k).wait_recv()

        @pl.when(c == 1)
        def _():
            col_in(stream).wait_recv()

    def drain(stream):
        for i in range(rows):

            @pl.when(jnp.logical_or(c == 1, k != i))
            def _():
                row_out(stream, i).wait_send()

        @pl.when(c == 0)
        def _():
            col_out(stream).wait_send()

    pl.semaphore_wait(barrier, total - 1)
    weights = remote(w_hbm, wb, w_sem.at[0], w_sem.at[1], k, 1 - c)
    launch(streams[0])
    launch(streams[1])
    weights.start()
    loads[-1].wait()
    for i in range(rows):
        gs[i] = (cot_ref[i].astype(jnp.float32) * hidden_t[:, i : i + 1]).astype(jnp.bfloat16)
    launch(streams[2])

    for row_src, col_src, dst, _, _ in streams:

        @pl.when(c == 1)
        def _():
            dst[pl.ds(rows, rows)] = col_src[...]

        for i in range(rows):

            @pl.when(jnp.logical_and(c == 0, k == i))
            def _():
                dst[i] = row_src[i]

    t_at = lax.broadcasted_iota(jnp.int32, (toks, toks), 0)
    k_at = lax.broadcasted_iota(jnp.int32, (toks, toks), 1)
    step = jnp.where(c == 0, 1, cols)
    mask = jnp.logical_and(t_at >= k_at, lax.rem(t_at, step) == lax.rem(k_at, step))
    low = lax.broadcasted_iota(jnp.int32, (toks, 128), 1) < N

    arrive(streams[1])
    ones = mask.astype(jnp.float32)
    dec = jnp.concatenate([db[i] for i in range(chips)], axis=1)
    run_s = lax.dot_general(ones, dec, NT, precision=PRECISE, preferred_element_type=jnp.float32)
    run_l = lax.dot_general(dec, ones, NT, precision=PRECISE, preferred_element_type=jnp.float32)
    heads = dec.shape[0]
    for h in range(heads):
        gap = run_s[:, h : h + 1] - run_l[h : h + 1, :]
        dec_s[h] = jnp.where(mask, jnp.exp(jnp.minimum(gap, 0.0)), 0.0)

    load_w.wait()
    arrive(streams[0])
    mine, rest = pl.multiple_of(c * part, part), pl.multiple_of((1 - c) * part, part)
    own = xb[:, :, pl.ds(mine, part)].reshape(toks, part)
    oth = xb[:, :, pl.ds(rest, part)].reshape(toks, part)
    pieces = ((u_s, c * half, half), (z_s, 2 * half + c * half, half), (bc_s, 4 * half + c * 2 * N, 2 * N))
    partial = [
        mm(own, wa[pl.ds(pl.multiple_of(start, 128), size), :], NT) for _, start, size in pieces
    ]
    weights.wait_recv()
    for (dst, start, size), first in zip(pieces, partial):
        second = mm(oth, wb[pl.ds(pl.multiple_of(start, 128), size), :], NT)
        dst[...] = (first + second).astype(jnp.bfloat16)

    b_bf, c_bf = bc_s[:, :N], bc_s[:, N:]
    scores = mm(c_bf, b_bf, NT)

    def per_head(x):
        first = jnp.sum(jnp.where(low, x, 0.0), axis=1, keepdims=True)
        second = jnp.sum(jnp.where(low, 0.0, x), axis=1, keepdims=True)
        return jnp.where(low, first, second) * (1.0 / N)

    def norm(p):
        cols_p = slice(p * 128, (p + 1) * 128)
        z = z_s[:, cols_p].astype(jnp.float32)
        sig_z = 1.0 / (1.0 + jnp.exp(-z))
        y = y_s[:, cols_p]
        gated = y * (z * sig_z)
        inv = lax.rsqrt(per_head(gated * gated) + EPSILON)
        return cols_p, z, sig_z, y, inv, gated * inv

    for p in range(half // 128):
        cols_p = slice(p * 128, (p + 1) * 128)
        u = u_s[:, cols_p].astype(jnp.float32)
        val_bf = (u / (1.0 + jnp.exp(-u))).astype(jnp.bfloat16)
        for h in (2 * p, 2 * p + 1):
            mat_s[h] = (dec_s[h] * scores).astype(jnp.bfloat16)
        y_s[:, cols_p] = jnp.where(
            low, mm(mat_s[2 * p], val_bf, NN), mm(mat_s[2 * p + 1], val_bf, NN)
        )
        normed_s[:, cols_p] = norm(p)[-1].astype(jnp.bfloat16)

    load_o.wait()
    arrive(streams[2])

    def weight_block(chip):
        at = pl.ds(pl.multiple_of(chip * 128, 128), 128)
        return mm(gb[:, :, at].reshape(toks, 128), normed_s[...], TN)

    def across(q):
        return remote(xsend.at[q], xr.at[q], xr_send.at[q], xr_recv.at[q], 2 * zi + 1 - xi, c)

    far = sorted(range(1, depth), key=lambda j: -min(j, depth - j)) + [0]
    order = [lax.rem(zi + j, depth) for j in far]
    for q in order:
        xsend[q] = weight_block(2 * q + 1 - xi).astype(jnp.bfloat16)
        across(q).start()

    grads = gb[...].reshape(toks, feat)
    gn_s[...] = mm(grads, wout[...], NN).astype(jnp.bfloat16)
    d_scores = jnp.zeros((toks, toks), jnp.float32)
    for p in range(half // 128):
        cols_p, z, sig_z, y, inv, normed = norm(p)
        u = u_s[:, cols_p].astype(jnp.float32)
        sig_u = 1.0 / (1.0 + jnp.exp(-u))
        val_bf = (u * sig_u).astype(jnp.bfloat16)
        gn = gn_s[:, cols_p].astype(jnp.float32)
        gg = inv * (gn - normed * per_head(gn * normed))
        dy = gg * (z * sig_z)
        dz = gg * y * (sig_z * (1.0 + z * (1.0 - sig_z)))
        dy_bf = dy.astype(jnp.bfloat16)
        dv = jnp.where(low, mm(mat_s[2 * p], dy_bf, TN), mm(mat_s[2 * p + 1], dy_bf, TN))
        du = dv * (sig_u * (1.0 + u * (1.0 - sig_u)))
        gp[:, :, cols_p] = du.astype(jnp.bfloat16).reshape(chips, cols, 128)
        gp[:, :, half + p * 128 : half + (p + 1) * 128] = dz.astype(jnp.bfloat16).reshape(
            chips, cols, 128
        )
        zero = jnp.zeros_like(dy)
        d_scores += dec_s[2 * p] * mm(jnp.where(low, dy, zero).astype(jnp.bfloat16), val_bf, NT)
        d_scores += dec_s[2 * p + 1] * mm(jnp.where(low, zero, dy).astype(jnp.bfloat16), val_bf, NT)
    ds_bf = d_scores.astype(jnp.bfloat16)
    d_bc = jnp.concatenate([mm(ds_bf, c_bf, TN), mm(ds_bf, b_bf, NN)], axis=1)
    gp[:, :, 2 * half :] = d_bc.astype(jnp.bfloat16).reshape(chips, cols, 2 * N)

    home, slot = k // rows, lax.rem(k, rows)

    def row_back(chip):
        return remote(gp.at[chip], grow.at[slot], gp_send.at[chip], gp_recv.at[slot], chip, home)

    def col_back(core):
        lo = pl.ds(0, rows)
        return remote(gp.at[lo], gcol, gp_send.at[chips], gp_recv.at[rows], k, core)

    @pl.when(c == 0)
    def _():
        for d in sorted(range(1, chips), key=lambda j: -min(j, chips - j)):
            row_back(lax.rem(k + d, chips)).start()

        @pl.when(home == 1)
        def _():
            row_back(k).start()

        for i in range(rows):

            @pl.when(k == i)
            def _():
                grow[i] = gp[i]

    @pl.when(c == 1)
    def _():
        col_back(0).start()
        gcol[...] = gp[pl.ds(rows, rows)]

    for q in range(depth):
        wgo[q] = weight_block(2 * q + xi)

    def along(q, core):
        return remote(
            zs.at[q, core], zr.at[zi, c], z_send.at[2 * q + core], z_recv.at[2 * zi + c], 2 * q + xi, core
        )

    def forward(q):
        across(q).wait_recv()
        both = wgo[q] + xr[q].astype(jnp.float32)
        wgo[q] = both
        zs[q] = both.astype(jnp.bfloat16).reshape(2, both.shape[0] // 2, both.shape[1])

    def forward_far(q):
        forward(q)
        for core in range(2):
            along(q, core).start()

    def back_project(src, g, w_ref):
        flat = src[...].reshape(rows * cols, 2 * half + 2 * N)
        acc = mm(flat[:, :half], w_ref[g * half : (g + 1) * half, :], NN)
        acc += mm(flat[:, half : 2 * half], w_ref[(2 + g) * half : (3 + g) * half, :], NN)
        at = 4 * half + g * 2 * N
        return acc + mm(flat[:, 2 * half :], w_ref[at : at + 2 * N, :], NN)

    forward_far(order[0])

    @pl.when(c == 0)
    def _():
        col_back(1).wait_recv()

    col_part = [back_project(gcol, 1, w_ref) for w_ref in (wa, wb)]
    for q in order[1:-1]:
        forward_far(q)
    forward(zi)
    along(zi, 1 - c).start()

    for i in range(rows):

        @pl.when(jnp.logical_or(c == 1, k != i))
        def _():
            remote(gp.at[0], grow.at[i], gp_send.at[0], gp_recv.at[i], k, 1 - c).wait_recv()

    for w_ref, at, first in ((wa, mine, col_part[0]), (wb, rest, col_part[1])):
        acc = (first + back_project(grow, 0, w_ref)).reshape(rows, cols, part)
        for i in range(rows):
            keep = present_t[:, i : i + 1] * (1.0 - hidden_t[:, i : i + 1])
            pg_ref[i, :, pl.ds(at, part)] = (acc[i] * keep).astype(pg_ref.dtype)

    for q in order[:-1]:
        for core in range(2):
            remote(zs.at[0, 0], zr.at[q, core], z_send.at[0], z_recv.at[2 * q + core], k, 1 - c).wait_recv()
    remote(zs.at[0, 0], zr.at[zi, 1 - c], z_send.at[0], z_recv.at[2 * zi + 1 - c], k, 1 - c).wait_recv()
    zr[zi, c] = zs[zi, c]
    for core in range(2):
        acc = zr[0, core].astype(jnp.float32)
        for q in range(1, depth):
            acc += zr[q, core].astype(jnp.float32)
        out_ref[:, core * half : (core + 1) * half] = acc * scale

    for stream in streams:
        drain(stream)
    weights.wait_send()
    for q in order:
        across(q).wait_send()
    for q in order[:-1]:
        for core in range(2):
            along(q, core).wait_send()
    along(zi, 1 - c).wait_send()

    @pl.when(c == 0)
    def _():
        for d in range(1, chips):
            row_back(lax.rem(k + d, chips)).wait_send()

        @pl.when(home == 1)
        def _():
            row_back(k).wait_send()

    @pl.when(c == 1)
    def _():
        col_back(0).wait_send()


def owned(
    patches, mask_token, masked, tissue, in_weight, out_weight, row_decay, col_decay, cotangent
):
    rows, cols, feat = patches.shape
    chips = lax.axis_size("gcol")
    toks, heads = chips * cols, row_decay.shape[0]
    half, part = out_weight.shape[1], in_weight.shape[1]
    width = 2 * half + 2 * N
    slab = feat // (2 * chips)
    depth = chips // 2
    bf, fl = jnp.bfloat16, jnp.float32
    vmem, dma = pltpu.VMEM, pltpu.SemaphoreType.DMA
    in_vmem, anywhere = pl.BlockSpec(memory_space=pltpu.VMEM), pl.BlockSpec(memory_space=pltpu.HBM)
    scale = 1.0 / math.sqrt(2 * rows * cols * chips)
    return pl.pallas_call(
        functools.partial(layer_kernel, chips, rows, scale),
        name="layer",
        out_shape=(
            jax.ShapeDtypeStruct(patches.shape, bf),
            jax.ShapeDtypeStruct((slab, 2 * half), fl),
        ),
        in_specs=[anywhere] * 9,
        out_specs=(in_vmem, in_vmem),
        scratch_shapes=[
            vmem(patches.shape, bf), vmem(mask_token.shape, bf), vmem(patches.shape, bf),
            vmem(masked.shape, masked.dtype), vmem(tissue.shape, tissue.dtype),
            vmem(row_decay.shape, fl), vmem(col_decay.shape, fl), dma((7,)),
            vmem((rows, cols, feat), bf), vmem((rows, cols, feat), bf),
            vmem((rows, heads, cols), fl), vmem((rows, heads, cols), fl),
            vmem((chips, cols, feat), bf), vmem((chips, cols, feat), bf), vmem((chips, heads, cols), fl),
            vmem(in_weight.shape, bf), vmem(in_weight.shape, bf), vmem(out_weight.shape, bf),
            vmem((toks, half), bf), vmem((toks, half), bf), vmem((toks, half), bf),
            vmem((toks, 2 * N), bf), vmem((toks, half), bf), vmem((toks, half), fl),
            vmem((heads, toks, toks), bf), vmem((heads, toks, toks), fl),
            vmem((chips, cols, width), bf), vmem((rows, cols, width), bf), vmem((rows, cols, width), bf),
            vmem((depth, 2 * slab, half), bf), vmem((depth, 2 * slab, half), fl),
            vmem((depth, 2 * slab, half), bf), vmem((depth, 2, slab, half), bf),
            vmem((depth, 2, slab, half), bf),
            dma((rows + 1,)), dma((chips + 1,)), dma((rows + 1,)), dma((chips + 1,)),
            dma((rows + 1,)), dma((chips + 1,)), dma((2,)), dma((2,)),
            dma((chips + 1,)), dma((rows + 1,)), dma((depth,)), dma((depth,)),
            dma((2 * depth,)), dma((2 * depth,)),
        ],
        compiler_params=pltpu.CompilerParams(
            collective_id=0, has_side_effects=True, vmem_limit_bytes=60 << 20
        ),
    )(
        patches, mask_token, cotangent, masked, tissue, row_decay, col_decay,
        in_weight, out_weight,
    )


def body(*args):
    rows = args[0].shape[0]
    if lax.axis_size("grow") == 2 and lax.axis_size("gcol") == 2 * rows:
        return owned(*args)
    return shards(*args)


def solution(mesh):
    return jax.shard_map(
        body,
        mesh=mesh,
        in_specs=(
            P(("groups", "grow"), "gcol", None),
            P(),
            P(("groups", "grow"), "gcol"),
            P(("groups", "grow"), "gcol"),
            P(None, "grow"),
            P(None, "grow"),
            P(None, ("groups", "grow"), "gcol"),
            P(None, ("groups", "grow"), "gcol"),
            P(("groups", "grow"), "gcol", None),
        ),
        out_specs=(P(("groups", "grow"), "gcol", None), P(("groups", "gcol", "grow"), None)),
        check_vma=False,
    )
```
